32 devices in a mesh: seq: 8 (over z, y), tp: 4 (over x, core).
Axes of the slice: x: 2, y: 2, z: 4, core: 2. Of those that a mesh axis runs over, the one named last changes fastest.
Arguments:
- hidden_in: bfloat16 [32, 4, 2048], replicated, may hold values from -6 to 6
- key_cache: bfloat16 [32, 1024, 1024], P(None, 'seq', 'tp'), may hold values from -256 to 256
- value_cache: bfloat16 [32, 1024, 1024], P(None, 'seq', 'tp'), may hold values from -6 to 6
- cache_len: int32 [32], replicated, may hold values from 1 to 1024, as said below
- sink_count: int32 [32], replicated, may hold values from 1 to 4, as said below
- attn_gain: bfloat16 [2048], replicated, may hold values from 0.099609375 to 1.8984375
- w_query: bfloat16 [2048, 2048], P(None, 'tp'), may hold values from -0.125 to 0.125
- w_key: bfloat16 [2048, 1024], P(None, 'tp'), may hold values from -0.125 to 0.125
- w_value: bfloat16 [2048, 1024], P(None, 'tp'), may hold values from -0.125 to 0.125
- w_headgate: bfloat16 [2048, 16], P(None, 'tp'), may hold values from -0.125 to 0.125
- q_gain: bfloat16 [128], replicated, may hold values from 0.25 to 1.75
- k_gain: bfloat16 [128], replicated, may hold values from 0.25 to 1.75
- w_output: bfloat16 [2048, 2048], P('tp'), may hold values from -0.5 to 0.5
Outputs:
- hidden_out: bfloat16 [32, 4, 2048], P(None, None, 'seq')
The draws below stay inside these ranges and needn't reach their ends.
Inputs may be any that keep to these rules, and one draw needn't show every extreme that they name: `cache_len`: some request has exactly 1024 cached positions and some exactly 1. `sink_count`: some request has exactly 4 sink positions and some exactly 1.
All inputs are finite; a program needn't handle non-finite values.
Results may differ from the reference program's by a relative error of at most 0.012.
The reference program's roundings to bfloat16 on the way count: a program that leaves them out, or rounds other values in their place, can miss the bound.
Values sent between devices are 32-bit elements; how exact they have to be, the bound alone decides.
A program may use at most 128 MiB of HBM per device.

```python
import jax
import jax.numpy as jnp
from jax import lax

D = 2048
QH = 16
KVH = 8
HD = 128
REQ = 32
NEW = 4
SINK_MAX = 4
CACHE = 1024
WIN = 512


def length_draw(key):
    first_key = jax.random.fold_in(key, 11)
    second_key = jax.random.fold_in(key, 12)
    drawn = jax.random.randint(first_key, (REQ,), 1, CACHE + 1)
    shuffled = jax.random.permutation(second_key, REQ)
    drawn = drawn.at[shuffled[0]].set(CACHE)
    drawn = drawn.at[shuffled[1]].set(1)
    return drawn.astype(jnp.int32)


def draw_cache_len(key, part):
    return length_draw(key)


def draw_sink_count(key, part):
    first_key = jax.random.fold_in(key, 21)
    second_key = jax.random.fold_in(key, 22)
    drawn = jax.random.randint(first_key, (REQ,), 1, SINK_MAX + 1)
    shuffled = jax.random.permutation(second_key, REQ)
    drawn = drawn.at[shuffled[0]].set(SINK_MAX)
    drawn = drawn.at[shuffled[1]].set(1)
    return drawn.astype(jnp.int32)


def draw_key_cache(key, part):
    noise_key = jax.random.fold_in(key, 31)
    noise = jax.random.truncated_normal(noise_key, -6.0, 6.0, (REQ, CACHE, KVH, HD), jnp.float32)
    sink_rows = (jnp.arange(CACHE, dtype=jnp.int32) < SINK_MAX)[None, :, None, None]
    drawn = noise * jnp.where(sink_rows, 8.0, 2.0)
    return drawn.reshape(REQ, CACHE, KVH * HD).astype(jnp.bfloat16)


def shard_levels(key, extent, cuts, smallest, top_value):
    loudness = 1.0
    for axis_at, blocks in cuts:
        steps = jax.random.uniform(jax.random.fold_in(jax.random.fold_in(key, 6), axis_at), (blocks,), jnp.float32, smallest / len(cuts), top_value / len(cuts))
        loudness = loudness * jnp.repeat(jnp.exp(steps), extent[axis_at] // blocks).reshape((-1,) + (1,) * (len(extent) - 1 - axis_at))
    return loudness


def scatter_about(rng, dims, width, bound, cuts=(), kind=jnp.bfloat16):
    entries = jax.random.normal(rng, dims, jnp.float32) * width
    if len(cuts) > 0:
        entries = shard_levels(rng, dims, cuts, -0.22, 0.18) * entries
    return jnp.clip(entries, min=-bound, max=bound).astype(kind)


def setup_inputs(seed: int = 0) -> dict:
    key_of = jax.random.split(jax.random.key(seed), 14)
    hidden_in = scatter_about(key_of[0], (REQ, NEW, D), 1.0, 6.0)
    key_cache = draw_key_cache(jax.random.fold_in(key_of[13], 71), 0)
    value_cache = scatter_about(key_of[2], (REQ, CACHE, KVH * HD), 1.0, 6.0, ((1, 8), (2, 4)))
    cache_len = draw_cache_len(jax.random.fold_in(key_of[13], 71), 0)
    sink_count = draw_sink_count(jax.random.fold_in(key_of[13], 71), 0)
    attn_gain = jnp.clip(1.0 + 0.18 * jax.random.normal(key_of[5], (D,), jnp.float32), 0.099609375, 1.8984375).astype(jnp.bfloat16)
    w_query = scatter_about(key_of[6], (D, QH * HD), D ** -0.5, 0.125, ((1, 4),))
    w_key = scatter_about(key_of[7], (D, KVH * HD), D ** -0.5, 0.125, ((1, 4),))
    w_value = scatter_about(key_of[8], (D, KVH * HD), D ** -0.5, 0.125, ((1, 4),))
    w_headgate = scatter_about(key_of[9], (D, QH), D ** -0.5, 0.125, ((1, 4),))
    q_gain = jnp.clip(1.0 + 0.15 * jax.random.normal(key_of[10], (HD,), jnp.float32), 0.25, 1.75).astype(jnp.bfloat16)
    k_gain = jnp.clip(1.0 + 0.15 * jax.random.normal(key_of[11], (HD,), jnp.float32), 0.25, 1.75).astype(jnp.bfloat16)
    w_output = scatter_about(key_of[12], (QH * HD, D), (QH * HD // 16) ** -0.5, 0.5, ((0, 4),))
    return dict(hidden_in=hidden_in, key_cache=key_cache, value_cache=value_cache, cache_len=cache_len, sink_count=sink_count, attn_gain=attn_gain, w_query=w_query, w_key=w_key, w_value=w_value, w_headgate=w_headgate, q_gain=q_gain, k_gain=k_gain, w_output=w_output)


rope_theta = 1000000.0
norm_eps = 1e-06
masked_fill = -1e+30

def rms_scale(values, gain_vec):
    mean_sq = lax.optimization_barrier(jnp.mean(values * values, axis=-1, keepdims=True))
    return values * lax.rsqrt(mean_sq + norm_eps) * gain_vec.astype(jnp.float32)

def rotate(values, positions):
    half_dim = values.shape[-1] // 2
    inv_freq = rope_theta ** (-jnp.arange(half_dim, dtype=jnp.float32) * 2.0 / values.shape[-1])
    phases = positions.astype(jnp.float32)[:, None] * inv_freq[None, :]
    cosine = jnp.cos(phases)[:, None, :]
    sine_term = jnp.sin(phases)[:, None, :]
    lower_half = values[..., :half_dim]
    upper_half = values[..., half_dim:]
    return jnp.concatenate([lower_half * cosine - upper_half * sine_term, upper_half * cosine + lower_half * sine_term], axis=-1)

def finish_heads(query, new_keys, new_values, gate_logit, positions, q_gain, k_gain):
    row_count = query.shape[0]
    head_dim = q_gain.shape[0]
    query_heads = rotate(rms_scale(query.reshape(row_count, -1, head_dim), q_gain), positions)
    key_heads = rotate(rms_scale(new_keys.reshape(row_count, -1, head_dim), k_gain), positions)
    return (query_heads.reshape(row_count, -1).astype(jnp.bfloat16), key_heads.reshape(row_count, -1).astype(jnp.bfloat16), new_values.astype(jnp.bfloat16), jax.nn.sigmoid(gate_logit).astype(jnp.bfloat16))

def reference(hidden_in, key_cache, value_cache, cache_len, sink_count, attn_gain, w_query, w_key, w_value, w_headgate, q_gain, k_gain, w_output):
    row_count = REQ * NEW
    per_group = QH // KVH
    residual = hidden_in.reshape(row_count, D).astype(jnp.float32)
    normed = (residual * lax.rsqrt(lax.optimization_barrier(jnp.mean(residual * residual, axis=1)) + norm_eps)[:, None] * attn_gain.astype(jnp.float32)).astype(jnp.bfloat16)
    positions = (cache_len[:, None] + jnp.arange(NEW, dtype=jnp.int32)[None, :]).reshape(row_count)
    query, new_keys, new_values, head_gate = finish_heads(jnp.dot(normed, w_query, preferred_element_type=jnp.float32), jnp.dot(normed, w_key, preferred_element_type=jnp.float32), jnp.dot(normed, w_value, preferred_element_type=jnp.float32), jnp.dot(normed, w_headgate, preferred_element_type=jnp.float32), positions, q_gain, k_gain)
    query_grid = query.reshape(REQ, NEW, KVH, per_group, HD)
    key_grid = new_keys.reshape(REQ, NEW, KVH, HD)
    value_grid = new_values.reshape(REQ, NEW, KVH, HD)

    def one_request(inputs):
        query_row, key_row, value_row, key_store, value_store, length, sink_size = inputs
        scaling = HD ** (-0.5)
        query_f32 = query_row.astype(jnp.float32)
        key_rows = key_store.reshape(CACHE, KVH, HD).astype(jnp.float32)
        value_rows = value_store.reshape(CACHE, KVH, HD).astype(jnp.float32)
        cache_scores = jnp.einsum('tkgd,ckd->kgtc', query_f32, key_rows, precision=lax.Precision.HIGHEST) * scaling
        fresh_scores = jnp.einsum('tkgd,jkd->kgtj', query_f32, key_row.astype(jnp.float32), precision=lax.Precision.HIGHEST) * scaling
        cache_pos = jnp.arange(CACHE, dtype=jnp.int32)
        newest_pos = length + jnp.arange(NEW, dtype=jnp.int32)
        allow_cache = (cache_pos[None, :] < length) & ((cache_pos[None, :] < sink_size) | (newest_pos[:, None] - cache_pos[None, :] < WIN))
        allow_fresh = jnp.arange(NEW, dtype=jnp.int32)[None, :] <= jnp.arange(NEW, dtype=jnp.int32)[:, None]
        scores = jnp.concatenate([cache_scores, fresh_scores], axis=-1)
        allowed = jnp.concatenate([allow_cache, allow_fresh], axis=-1)[None, None, :, :]
        top_score = lax.optimization_barrier(jnp.max(jnp.where(allowed, scores, masked_fill), axis=-1))
        weights = jnp.where(allowed, jnp.exp(scores - top_score[..., None]), 0.0)
        weight_sum = lax.optimization_barrier(jnp.sum(weights, axis=-1))
        rounded = lax.optimization_barrier(weights.astype(jnp.bfloat16)).astype(jnp.float32)
        value_all = jnp.concatenate([value_rows, value_row.astype(jnp.float32)], axis=0)
        weighted = jnp.einsum('kgtc,ckd->kgtd', rounded, value_all, precision=lax.Precision.HIGHEST)
        return weighted / weight_sum[..., None]
    attended = lax.map(one_request, (query_grid, key_grid, value_grid, key_cache, value_cache, cache_len, sink_count))
    attended = jnp.transpose(attended, (0, 3, 1, 2, 4)).reshape(row_count, QH, HD)
    gated = (attended * head_gate.astype(jnp.float32)[:, :, None]).astype(jnp.bfloat16).reshape(row_count, QH * HD)
    projected = jnp.dot(gated, w_output, preferred_element_type=jnp.float32)
    return (residual + projected).astype(jnp.bfloat16).reshape(REQ, NEW, D)
```

```python
import functools

import jax
import jax.numpy as jnp
import numpy as np
from jax import lax
from jax.experimental import pallas as pl
from jax.experimental.pallas import tpu as pltpu
from jax.sharding import PartitionSpec as P

rope_theta = 1000000.0
norm_eps = 1e-06
masked_fill = -1e30


def rms_scale(values, gain_vec):
    mean_sq = jnp.mean(values * values, axis=-1, keepdims=True)
    return values * lax.rsqrt(mean_sq + norm_eps) * gain_vec.astype(jnp.float32)


def rotate(values, positions):
    half_dim = values.shape[-1] // 2
    inv_freq = rope_theta ** (-jnp.arange(half_dim, dtype=jnp.float32) * 2.0 / values.shape[-1])
    phases = positions.astype(jnp.float32)[:, None] * inv_freq[None, :]
    cosine = jnp.cos(phases)[:, None, :]
    sine_term = jnp.sin(phases)[:, None, :]
    lower_half = values[..., :half_dim]
    upper_half = values[..., half_dim:]
    return jnp.concatenate(
        [
            lower_half * cosine - upper_half * sine_term,
            upper_half * cosine + lower_half * sine_term,
        ],
        axis=-1,
    )


def finish_heads(query, new_keys, new_values, gate_logit, positions, q_gain, k_gain):
    row_count = query.shape[0]
    head_dim = q_gain.shape[0]
    query_heads = rotate(rms_scale(query.reshape(row_count, -1, head_dim), q_gain), positions)
    key_heads = rotate(rms_scale(new_keys.reshape(row_count, -1, head_dim), k_gain), positions)
    return (
        query_heads.reshape(row_count, -1).astype(jnp.bfloat16),
        key_heads.reshape(row_count, -1).astype(jnp.bfloat16),
        new_values.astype(jnp.bfloat16),
        jax.nn.sigmoid(gate_logit).astype(jnp.bfloat16),
    )


def softmax_part(scores, allowed, value_rows, form):
    top_score = jnp.max(jnp.where(allowed, scores, masked_fill), axis=-1)
    weights = jnp.where(allowed, jnp.exp(scores - top_score[..., None]), 0.0)
    weight_sum = jnp.sum(weights, axis=-1)
    weighted = jnp.einsum(
        form, weights.astype(jnp.bfloat16), value_rows, preferred_element_type=jnp.float32
    )
    return (top_score, weight_sum, weighted)


def join_parts(first_part, second_part):
    top_score = jnp.maximum(first_part[0], second_part[0])
    left_scale = jnp.exp(first_part[0] - top_score)
    right_scale = jnp.exp(second_part[0] - top_score)
    return (
        top_score,
        first_part[1] * left_scale + second_part[1] * right_scale,
        first_part[2] * left_scale[..., None] + second_part[2] * right_scale[..., None],
    )


def piece_attention(queries, cache_keys, cache_values, lengths, sinks, offset, window):
    req_count, slot_count = (cache_keys.shape[0], cache_keys.shape[1])
    kv_heads, head_dim = (queries.shape[2], queries.shape[4])
    key_rows = cache_keys.reshape(req_count, slot_count, kv_heads, head_dim)
    value_rows = cache_values.reshape(req_count, slot_count, kv_heads, head_dim)
    scores = jnp.einsum(
        "rtkgd,rskd->rkgts", queries, key_rows, preferred_element_type=jnp.float32
    ) * head_dim ** (-0.5)
    cache_pos = offset + jnp.arange(slot_count, dtype=jnp.int32)
    newest_pos = lengths[:, None] + jnp.arange(queries.shape[1], dtype=jnp.int32)[None, :]
    allowed = (cache_pos[None, None, :] < lengths[:, None, None]) & (
        (cache_pos[None, None, :] < sinks[:, None, None])
        | (newest_pos[:, :, None] - cache_pos[None, None, :] < window)
    )
    return softmax_part(scores, allowed[:, None, None, :, :], value_rows, "rkgts,rskd->rkgtd")


def plain_device(
    hidden_in,
    key_cache,
    value_cache,
    cache_len,
    sink_count,
    attn_gain,
    w_query,
    w_key,
    w_value,
    w_headgate,
    q_gain,
    k_gain,
    w_output,
):
    req_count, new_count, model_width = hidden_in.shape
    head_dim = q_gain.shape[0]
    seq_count = lax.axis_size("seq")
    seq_rank = lax.axis_index("seq")
    row_count = req_count * new_count
    window = key_cache.shape[1] * seq_count // 2
    residual = hidden_in.reshape(row_count, model_width).astype(jnp.float32)
    normed = (
        residual
        * lax.rsqrt(jnp.mean(residual * residual, axis=1) + norm_eps)[:, None]
        * attn_gain.astype(jnp.float32)
    ).astype(jnp.bfloat16)
    positions = (cache_len[:, None] + jnp.arange(new_count, dtype=jnp.int32)[None, :]).reshape(
        row_count
    )
    query, new_keys, new_values, head_gate = finish_heads(
        jnp.dot(normed, w_query, preferred_element_type=jnp.float32),
        jnp.dot(normed, w_key, preferred_element_type=jnp.float32),
        jnp.dot(normed, w_value, preferred_element_type=jnp.float32),
        jnp.dot(normed, w_headgate, preferred_element_type=jnp.float32),
        positions,
        q_gain,
        k_gain,
    )
    kv_local = new_keys.shape[1] // head_dim
    q_local = query.shape[1] // head_dim
    per_group = q_local // kv_local
    query_grid = query.reshape(req_count, new_count, kv_local, per_group, head_dim)
    offset = seq_rank * key_cache.shape[1]
    cache_part = piece_attention(
        query_grid, key_cache, value_cache, cache_len, sink_count, offset, window
    )
    top_score = lax.pmax(cache_part[0], "seq")
    rescale = jnp.exp(cache_part[0] - top_score)
    weight_sum, weighted = lax.psum(
        (cache_part[1] * rescale, cache_part[2] * rescale[..., None]), "seq"
    )
    key_grid = new_keys.reshape(req_count, new_count, kv_local, head_dim)
    value_grid = new_values.reshape(req_count, new_count, kv_local, head_dim)
    fresh_scores = jnp.einsum(
        "rtkgd,rjkd->rkgtj", query_grid, key_grid, preferred_element_type=jnp.float32
    ) * head_dim ** (-0.5)
    causal_mask = (
        jnp.arange(new_count, dtype=jnp.int32)[None, :]
        <= jnp.arange(new_count, dtype=jnp.int32)[:, None]
    )
    fresh_part = softmax_part(
        fresh_scores, causal_mask[None, None, None, :, :], value_grid, "rkgtj,rjkd->rkgtd"
    )
    top_score, weight_sum, weighted = join_parts((top_score, weight_sum, weighted), fresh_part)
    attended = weighted / weight_sum[..., None]
    attended = jnp.transpose(attended, (0, 3, 1, 2, 4)).reshape(row_count, q_local, head_dim)
    gated = (
        (attended * head_gate.astype(jnp.float32)[:, :, None])
        .astype(jnp.bfloat16)
        .reshape(row_count, q_local * head_dim)
    )
    column_count = model_width // seq_count
    column_start = seq_rank * column_count
    residual_columns = lax.dynamic_slice_in_dim(residual, column_start, column_count, 1)
    projected = lax.psum(jnp.dot(gated, w_output, preferred_element_type=jnp.float32), "tp")
    projected_columns = lax.dynamic_slice_in_dim(projected, column_start, column_count, 1)
    finished_columns = (residual_columns + projected_columns).astype(jnp.bfloat16)
    return finished_columns.reshape(req_count, new_count, column_count)


def one_hot(flag):
    return jnp.where(flag, 1.0, 0.0).astype(jnp.bfloat16)


def iota(shape, axis):
    return lax.broadcasted_iota(jnp.int32, shape, axis)


def quot(values, size):
    return lax.shift_right_logical(values, size.bit_length() - 1)


def rest(values, size):
    return values & (size - 1)


def head_vectors(sums, gain, cosine, sine):
    scale = lax.rsqrt(jnp.mean(sums * sums, axis=-1, keepdims=True) + norm_eps)
    normed = sums * scale * gain
    turned = normed * cosine + pltpu.roll(normed, sums.shape[1] // 2, 1) * sine
    return turned.astype(jnp.bfloat16)


def attend(scores, allowed):
    top = jnp.max(jnp.where(allowed, scores, masked_fill), axis=-1, keepdims=True)
    weights = jnp.where(allowed, jnp.exp(scores - top), 0.0)
    return top, jnp.sum(weights, axis=-1, keepdims=True), weights.astype(jnp.bfloat16)


def store_part(ref, at, top, total, weighted):
    rows, lanes = weighted.shape
    ref[at, :rows, :] = weighted
    spread = iota((rows, lanes), 1) - iota((rows, lanes), 0)
    stats = jnp.where(spread == 0, top, 0.0) + jnp.where(spread == rows, total, 0.0)
    ref[at, pl.ds(rows, 1), :] = jnp.sum(stats, axis=0, keepdims=True)


def block_kernel(
    seq_count, tp_count, new_count, per_group,
    lens_ref, sinks_ref, freq_ref, hidden_ref, gain_ref, qg_ref, kg_ref, wg_ref,
    wq_hbm, wk_hbm, wv_hbm, wo_hbm, kc_hbm, vc_hbm,
    out_ref,
    wq_ref, wk_ref, wv_ref, wo_ref, kc_ref, vc_ref, placed_ref,
    part_ref, got, send_sum, got_sum, done, final,
    sems, s_send, s_recv, t_send, t_recv, f_send, f_recv,
):
    copies = []
    for n, (a, b) in enumerate(
        (
            (wq_hbm, wq_ref), (kc_hbm, kc_ref), (vc_hbm, vc_ref),
            (wk_hbm, wk_ref), (wv_hbm, wv_ref), (wo_hbm, wo_ref),
        )
    ):
        copies.append(pltpu.make_async_copy(a, b, sems.at[n]))
        copies[-1].start()
    copy_q, copy_kc, copy_vc, copy_k, copy_v, copy_o = copies
    rank = lax.axis_index("seq")
    t = lax.axis_index("tp")
    barrier = pltpu.get_barrier_semaphore()
    for ds in range(seq_count):
        for dt in range(tp_count):
            if ds or dt:
                pl.semaphore_signal(
                    barrier,
                    inc=1,
                    device_id={"seq": (rank + ds) % seq_count, "tp": (t + dt) % tp_count},
                    device_id_type=pl.DeviceIdType.MESH,
                )

    def remote(src, dst, send, recv, seq, tp):
        return pltpu.make_async_remote_copy(
            src_ref=src, dst_ref=dst, send_sem=send, recv_sem=recv,
            device_id={"seq": seq, "tp": tp}, device_id_type=pl.DeviceIdType.MESH,
        )

    reqs, slots, width = kc_ref.shape
    rows = reqs * new_count
    hd = freq_ref.shape[1]
    kv_heads = width // hd
    heads = kv_heads * per_group
    each = heads * new_count
    full = reqs * each
    own_reqs = reqs // seq_count
    own = own_reqs * each
    own_rows = own_reqs * new_count
    window = slots * seq_count // 2

    x = hidden_ref[...].astype(jnp.float32).reshape(rows, hidden_ref.shape[2])
    normed = (
        x
        * lax.rsqrt(jnp.mean(x * x, axis=1, keepdims=True) + norm_eps)
        * gain_ref[...].astype(jnp.float32).reshape(1, -1)
    ).astype(jnp.bfloat16)
    lens = lens_ref[...].astype(jnp.float32)
    sinks = sinks_ref[...].astype(jnp.float32)

    def per_row(values, count, size, base):
        chosen = base + quot(iota((count, reqs), 0), size) == iota((count, reqs), 1)
        return jnp.sum(jnp.where(chosen, values, 0.0), axis=1, keepdims=True)

    token = rest(iota((rows, 1), 0), new_count).astype(jnp.float32)
    place = per_row(lens, rows, new_count, 0) + token
    low = iota((rows // 2, hd), 1) < hd // 2
    angle = jnp.where(low, place[: rows // 2], place[rows // 2 :]) * freq_ref[...]

    def unpack(packed, sign):
        turned = pltpu.roll(packed, hd // 2, 1)
        first = jnp.where(low, sign * packed, turned)
        second = jnp.where(low, sign * turned, packed)
        return jnp.concatenate([first, second], axis=0)

    cosine = unpack(jnp.cos(angle), 1.0)
    sine = unpack(jnp.sin(angle), -1.0)
    q_gain = qg_ref[...].astype(jnp.float32)
    k_gain = kg_ref[...].astype(jnp.float32)

    copy_q.wait()
    q_sum = jnp.dot(normed, wq_ref[...], preferred_element_type=jnp.float32)
    query = [
        head_vectors(q_sum[:, h * hd : (h + 1) * hd], q_gain, cosine, sine) for h in range(heads)
    ]
    at = iota((full, rows), 0)
    source = quot(at, each) * new_count + rest(at, new_count)
    hit = source == iota((full, rows), 1)
    head_of = rest(quot(at, new_count), heads)
    for k in range(kv_heads):
        picks = [one_hot(hit & (head_of == k * per_group + g)) for g in range(per_group)]
        moved = jnp.dot(
            jnp.concatenate(picks, axis=1),
            jnp.concatenate(query[k * per_group : (k + 1) * per_group], axis=0),
            preferred_element_type=jnp.float32,
        )
        placed_ref[:, k * hd : (k + 1) * hd] = moved.astype(jnp.bfloat16)

    copy_kc.wait()
    copy_vc.wait()
    contract = (((1,), (1,)), ((), ()))
    group = each // kv_heads
    pos = rank * slots + iota((own, slots), 1)

    def piece(owner):
        first = owner * own_reqs
        queries = placed_ref[pl.ds(pl.multiple_of(owner * own, own), own), :]
        scores = [
            lax.dot_general(
                queries[r * each : (r + 1) * each],
                kc_ref[first + r],
                contract,
                preferred_element_type=jnp.float32,
            )
            for r in range(own_reqs)
        ]
        scores = jnp.concatenate(scores, axis=0) * hd ** (-0.5)
        length = per_row(lens, own, each, first).astype(jnp.int32)
        sink = per_row(sinks, own, each, first).astype(jnp.int32)
        newest = length + rest(iota((own, 1), 0), new_count)
        allowed = (pos < length) & ((pos < sink) | (newest - pos < window))
        top, total, probs = attend(scores, allowed)
        weighted = []
        for r in range(own_reqs):
            both = jnp.dot(
                probs[r * each : (r + 1) * each],
                vc_ref[first + r],
                preferred_element_type=jnp.float32,
            )
            for k in range(kv_heads):
                weighted.append(both[k * group : (k + 1) * group, k * hd : (k + 1) * hd])
        return top, total, jnp.concatenate(weighted, axis=0)

    half = seq_count // 2
    order = sorted(range(1, seq_count), key=lambda i: abs(i - half)) + [0]
    swaps = []
    for c in range(0, seq_count, 2):
        pair = order[c : c + 2]
        results = [piece((rank + i) % seq_count) for i in pair]
        for i, result in zip(pair, results):
            store_part(part_ref, i, *result)
        if c == 0:
            pl.semaphore_wait(barrier, seq_count * tp_count - 1)
        for i in pair:
            if i:
                copy = remote(
                    part_ref.at[i], got.at[i - 1], s_send.at[i - 1], s_recv.at[i - 1],
                    (rank + i) % seq_count, t,
                )
                copy.start()
                swaps.append((i, copy))

    copy_k.wait()
    k_sum = jnp.dot(normed, wk_ref[...], preferred_element_type=jnp.float32)
    keys = jnp.concatenate(
        [
            head_vectors(k_sum[:, k * hd : (k + 1) * hd], k_gain, cosine, sine)
            for k in range(kv_heads)
        ],
        axis=1,
    )
    copy_v.wait()
    values = jnp.dot(normed, wv_ref[...], preferred_element_type=jnp.float32).astype(jnp.bfloat16)
    mine = placed_ref[pl.ds(pl.multiple_of(rank * own, own), own), :]
    fresh = lax.dot_general(mine, keys, contract, preferred_element_type=jnp.float32)
    fresh = fresh * hd ** (-0.5)
    row = iota((own, rows), 0)
    col = iota((own, rows), 1)
    own_req = rank * own_reqs + quot(row, each)
    visible = (quot(col, new_count) == own_req) & (rest(col, new_count) <= rest(row, new_count))
    top, total, probs = attend(fresh, visible)
    both = jnp.dot(probs, values, preferred_element_type=jnp.float32)
    row_head = rest(quot(iota((own, hd), 0), new_count), heads)
    picked = jnp.zeros((own, hd), jnp.float32)
    for k in range(kv_heads):
        picked = jnp.where(quot(row_head, per_group) == k, both[:, k * hd : (k + 1) * hd], picked)
    store_part(part_ref, seq_count, top, total, picked)

    logits = lax.dot_general(normed, wg_ref[...], contract, preferred_element_type=jnp.float32)
    gates = jax.nn.sigmoid(logits).astype(jnp.bfloat16)
    pick = one_hot(col == own_req * new_count + rest(row, new_count))
    gates = jnp.dot(pick, gates, preferred_element_type=jnp.float32)
    small = (own, heads)
    gates = jnp.where(rest(quot(iota(small, 0), new_count), heads) == iota(small, 1), gates, 0.0)
    gate = jnp.sum(gates, axis=1, keepdims=True)

    row = iota((own_rows, own), 0)
    col = iota((own_rows, own), 1)
    base = quot(row, new_count) * each + rest(row, new_count)
    back = [one_hot(col == base + h * new_count) for h in range(heads)]
    copy_o.wait()

    pieces = [part_ref[0], part_ref[seq_count]]
    for i, copy in swaps:
        copy.wait_recv()
        pieces.append(got[i - 1])
    stats = [p[own : own + 1, :] for p in pieces]
    top = functools.reduce(jnp.maximum, stats)
    scales = [jnp.exp(jnp.minimum(p - top, 0.0)) for p in stats]
    total = functools.reduce(
        jnp.add, [pltpu.roll(p, own, 1) * scale for p, scale in zip(stats, scales)]
    )
    diagonal = iota((own, hd), 1) == iota((own, hd), 0)
    weighted = jnp.zeros((own, hd), jnp.float32)
    for p, scale in zip(pieces, scales):
        share = jnp.sum(jnp.where(diagonal, scale / total, 0.0), axis=1, keepdims=True)
        weighted = weighted + p[:own, :] * share
    gated = (weighted * gate).astype(jnp.bfloat16)
    lined = jnp.concatenate(
        [
            jnp.dot(b, gated, preferred_element_type=jnp.float32).astype(jnp.bfloat16)
            for b in back
        ],
        axis=1,
    )
    per = seq_count // tp_count
    cols = wo_ref.shape[1] // seq_count
    adds = []
    for i in list(range(1, tp_count)) + [0]:
        peer = (t + i) % tp_count
        for p in range(per):
            start = pl.multiple_of((p * tp_count + peer) * cols, cols)
            send_sum[i, p] = jnp.dot(
                lined, wo_ref[:, pl.ds(start, cols)], preferred_element_type=jnp.float32
            )
        if i:
            copy = remote(
                send_sum.at[i], got_sum.at[i - 1], t_send.at[i - 1], t_recv.at[i - 1], rank, peer
            )
            copy.start()
            adds.append(copy)
    reduced = send_sum[0]
    for i, copy in enumerate(adds):
        copy.wait_recv()
        reduced = reduced + got_sum[i]
    done[...] = reduced

    spreads = []
    for p in range(per):
        target = p * tp_count + t
        for dt in range(tp_count):
            n = p * tp_count + dt
            copy = remote(
                done.at[p], final.at[rank], f_send.at[n], f_recv.at[rank],
                target, (t + dt) % tp_count,
            )
            if dt:
                copy.start()
            else:

                @pl.when(target != rank)
                def _(copy=copy):
                    copy.start()

                @pl.when(target == rank)
                def _(p=p):
                    final[rank] = done[p]

            spreads.append((copy, target, dt))

    def arrival(i):
        src = (rank + i) % seq_count
        return remote(final.at[src], final.at[src], f_send.at[0], f_recv.at[src], src, rank % tp_count)

    def finish(i):
        src = (rank + i) % seq_count
        at = pl.ds(src * own_reqs, own_reqs)
        start = pl.multiple_of(rank * cols, cols)
        residual = hidden_ref[at, :, pl.ds(start, cols)].astype(jnp.float32)
        summed = final[src].reshape(own_reqs, new_count, cols)
        out_ref[at] = (residual + summed).astype(out_ref.dtype)

    @pl.when(t != rank % tp_count)
    def _():
        arrival(0).wait_recv()

    finish(0)
    for i in range(1, seq_count):
        arrival(i).wait_recv()
        finish(i)

    for copy in [c for _, c in swaps] + adds:
        copy.wait_send()
    for copy, target, dt in spreads:
        if dt:
            copy.wait_send()
        else:

            @pl.when(target != rank)
            def _(copy=copy):
                copy.wait_send()


def fits(seq_count, tp_count, reqs, new_count, heads, slots, hd, model_width):
    own = reqs // seq_count * heads * new_count
    return (
        reqs % seq_count == 0
        and seq_count % tp_count == 0
        and model_width % (128 * seq_count) == 0
        and own % 16 == 0
        and 2 * own == hd == slots == 128
        and reqs * new_count == 128
        and heads & (heads - 1) == 0
    )


def per_device(
    hidden_in, key_cache, value_cache, cache_len, sink_count, attn_gain,
    w_query, w_key, w_value, w_headgate, q_gain, k_gain, w_output,
):
    reqs, new_count, model_width = hidden_in.shape
    hd = q_gain.shape[0]
    slots, width = key_cache.shape[1:]
    seq_count = lax.axis_size("seq")
    tp_count = lax.axis_size("tp")
    heads = w_query.shape[1] // hd
    if not fits(seq_count, tp_count, reqs, new_count, heads, slots, hd, model_width):
        return plain_device(
            hidden_in, key_cache, value_cache, cache_len, sink_count, attn_gain,
            w_query, w_key, w_value, w_headgate, q_gain, k_gain, w_output,
        )
    each = heads * new_count
    own = reqs // seq_count * each
    freq = np.tile(rope_theta ** (-np.arange(hd // 2) * 2.0 / hd), 2)[None, :].astype(np.float32)
    vmem = pl.BlockSpec(memory_space=pltpu.VMEM)
    hbm = pl.BlockSpec(memory_space=pl.ANY)
    f32 = jnp.float32
    own_rows = own // heads
    cols = model_width // seq_count
    per = seq_count // tp_count
    sem = pltpu.SemaphoreType.DMA
    streamed = (w_query, w_key, w_value, w_output, key_cache, value_cache)
    return pl.pallas_call(
        functools.partial(block_kernel, seq_count, tp_count, new_count, heads * hd // width),
        out_shape=pltpu.VMEM((reqs, new_count, cols), hidden_in.dtype),
        in_specs=[vmem] * 8 + [hbm] * 6,
        out_specs=vmem,
        scratch_shapes=[pltpu.VMEM(a.shape, a.dtype) for a in streamed]
        + [
            pltpu.VMEM((reqs * each, width), jnp.bfloat16),
            pltpu.VMEM((seq_count + 1, own + 1, hd), f32),
            pltpu.VMEM((seq_count - 1, own + 1, hd), f32),
            pltpu.VMEM((tp_count, per, own_rows, cols), f32),
            pltpu.VMEM((tp_count - 1, per, own_rows, cols), f32),
            pltpu.VMEM((per, own_rows, cols), f32),
            pltpu.VMEM((seq_count, own_rows, cols), f32),
            sem((6,)),
            sem((seq_count - 1,)), sem((seq_count - 1,)),
            sem((tp_count - 1,)), sem((tp_count - 1,)),
            sem((seq_count,)), sem((seq_count,)),
        ],
        compiler_params=pltpu.CompilerParams(collective_id=0, has_side_effects=True),
        name="attention_block",
    )(
        cache_len[None, :], sink_count[None, :], freq, hidden_in, attn_gain,
        q_gain[None, :], k_gain[None, :], w_headgate.T, *streamed,
    )


def solution(mesh):
    placed = (
        P(),
        P(None, "seq", "tp"),
        P(None, "seq", "tp"),
        P(),
        P(),
        P(),
        P(None, "tp"),
        P(None, "tp"),
        P(None, "tp"),
        P(None, "tp"),
        P(),
        P(),
        P("tp", None),
    )
    return jax.shard_map(
        per_device, mesh=mesh, in_specs=placed, out_specs=P(None, None, "seq"), check_vma=False
    )
```

```python
import functools

import jax
import jax.numpy as jnp
import numpy as np
from jax import lax
from jax.experimental import pallas as pl
from jax.experimental.pallas import tpu as pltpu
from jax.sharding import PartitionSpec as P

rope_theta = 1000000.0
norm_eps = 1e-06
masked_fill = -1e30


def rms_scale(values, gain_vec):
    mean_sq = jnp.mean(values * values, axis=-1, keepdims=True)
    return values * lax.rsqrt(mean_sq + norm_eps) * gain_vec.astype(jnp.float32)


def rotate(values, positions):
    half_dim = values.shape[-1] // 2
    inv_freq = rope_theta ** (-jnp.arange(half_dim, dtype=jnp.float32) * 2.0 / values.shape[-1])
    phases = positions.astype(jnp.float32)[:, None] * inv_freq[None, :]
    cosine = jnp.cos(phases)[:, None, :]
    sine_term = jnp.sin(phases)[:, None, :]
    lower_half = values[..., :half_dim]
    upper_half = values[..., half_dim:]
    return jnp.concatenate(
        [
            lower_half * cosine - upper_half * sine_term,
            upper_half * cosine + lower_half * sine_term,
        ],
        axis=-1,
    )


def finish_heads(query, new_keys, new_values, gate_logit, positions, q_gain, k_gain):
    row_count = query.shape[0]
    head_dim = q_gain.shape[0]
    query_heads = rotate(rms_scale(query.reshape(row_count, -1, head_dim), q_gain), positions)
    key_heads = rotate(rms_scale(new_keys.reshape(row_count, -1, head_dim), k_gain), positions)
    return (
        query_heads.reshape(row_count, -1).astype(jnp.bfloat16),
        key_heads.reshape(row_count, -1).astype(jnp.bfloat16),
        new_values.astype(jnp.bfloat16),
        jax.nn.sigmoid(gate_logit).astype(jnp.bfloat16),
    )


def softmax_part(scores, allowed, value_rows, form):
    top_score = jnp.max(jnp.where(allowed, scores, masked_fill), axis=-1)
    weights = jnp.where(allowed, jnp.exp(scores - top_score[..., None]), 0.0)
    weight_sum = jnp.sum(weights, axis=-1)
    weighted = jnp.einsum(
        form, weights.astype(jnp.bfloat16), value_rows, preferred_element_type=jnp.float32
    )
    return (top_score, weight_sum, weighted)


def join_parts(first_part, second_part):
    top_score = jnp.maximum(first_part[0], second_part[0])
    left_scale = jnp.exp(first_part[0] - top_score)
    right_scale = jnp.exp(second_part[0] - top_score)
    return (
        top_score,
        first_part[1] * left_scale + second_part[1] * right_scale,
        first_part[2] * left_scale[..., None] + second_part[2] * right_scale[..., None],
    )


def piece_attention(queries, cache_keys, cache_values, lengths, sinks, offset, window):
    req_count, slot_count = (cache_keys.shape[0], cache_keys.shape[1])
    kv_heads, head_dim = (queries.shape[2], queries.shape[4])
    key_rows = cache_keys.reshape(req_count, slot_count, kv_heads, head_dim)
    value_rows = cache_values.reshape(req_count, slot_count, kv_heads, head_dim)
    scores = jnp.einsum(
        "rtkgd,rskd->rkgts", queries, key_rows, preferred_element_type=jnp.float32
    ) * head_dim ** (-0.5)
    cache_pos = offset + jnp.arange(slot_count, dtype=jnp.int32)
    newest_pos = lengths[:, None] + jnp.arange(queries.shape[1], dtype=jnp.int32)[None, :]
    allowed = (cache_pos[None, None, :] < lengths[:, None, None]) & (
        (cache_pos[None, None, :] < sinks[:, None, None])
        | (newest_pos[:, :, None] - cache_pos[None, None, :] < window)
    )
    return softmax_part(scores, allowed[:, None, None, :, :], value_rows, "rkgts,rskd->rkgtd")


def plain_device(
    hidden_in,
    key_cache,
    value_cache,
    cache_len,
    sink_count,
    attn_gain,
    w_query,
    w_key,
    w_value,
    w_headgate,
    q_gain,
    k_gain,
    w_output,
):
    req_count, new_count, model_width = hidden_in.shape
    head_dim = q_gain.shape[0]
    seq_count = lax.axis_size("seq")
    seq_rank = lax.axis_index("seq")
    row_count = req_count * new_count
    window = key_cache.shape[1] * seq_count // 2
    residual = hidden_in.reshape(row_count, model_width).astype(jnp.float32)
    normed = (
        residual
        * lax.rsqrt(jnp.mean(residual * residual, axis=1) + norm_eps)[:, None]
        * attn_gain.astype(jnp.float32)
    ).astype(jnp.bfloat16)
    positions = (cache_len[:, None] + jnp.arange(new_count, dtype=jnp.int32)[None, :]).reshape(
        row_count
    )
    query, new_keys, new_values, head_gate = finish_heads(
        jnp.dot(normed, w_query, preferred_element_type=jnp.float32),
        jnp.dot(normed, w_key, preferred_element_type=jnp.float32),
        jnp.dot(normed, w_value, preferred_element_type=jnp.float32),
        jnp.dot(normed, w_headgate, preferred_element_type=jnp.float32),
        positions,
        q_gain,
        k_gain,
    )
    kv_local = new_keys.shape[1] // head_dim
    q_local = query.shape[1] // head_dim
    per_group = q_local // kv_local
    query_grid = query.reshape(req_count, new_count, kv_local, per_group, head_dim)
    offset = seq_rank * key_cache.shape[1]
    cache_part = piece_attention(
        query_grid, key_cache, value_cache, cache_len, sink_count, offset, window
    )
    top_score = lax.pmax(cache_part[0], "seq")
    rescale = jnp.exp(cache_part[0] - top_score)
    weight_sum, weighted = lax.psum(
        (cache_part[1] * rescale, cache_part[2] * rescale[..., None]), "seq"
    )
    key_grid = new_keys.reshape(req_count, new_count, kv_local, head_dim)
    value_grid = new_values.reshape(req_count, new_count, kv_local, head_dim)
    fresh_scores = jnp.einsum(
        "rtkgd,rjkd->rkgtj", query_grid, key_grid, preferred_element_type=jnp.float32
    ) * head_dim ** (-0.5)
    causal_mask = (
        jnp.arange(new_count, dtype=jnp.int32)[None, :]
        <= jnp.arange(new_count, dtype=jnp.int32)[:, None]
    )
    fresh_part = softmax_part(
        fresh_scores, causal_mask[None, None, None, :, :], value_grid, "rkgtj,rjkd->rkgtd"
    )
    top_score, weight_sum, weighted = join_parts((top_score, weight_sum, weighted), fresh_part)
    attended = weighted / weight_sum[..., None]
    attended = jnp.transpose(attended, (0, 3, 1, 2, 4)).reshape(row_count, q_local, head_dim)
    gated = (
        (attended * head_gate.astype(jnp.float32)[:, :, None])
        .astype(jnp.bfloat16)
        .reshape(row_count, q_local * head_dim)
    )
    column_count = model_width // seq_count
    column_start = seq_rank * column_count
    residual_columns = lax.dynamic_slice_in_dim(residual, column_start, column_count, 1)
    projected = lax.psum(jnp.dot(gated, w_output, preferred_element_type=jnp.float32), "tp")
    projected_columns = lax.dynamic_slice_in_dim(projected, column_start, column_count, 1)
    finished_columns = (residual_columns + projected_columns).astype(jnp.bfloat16)
    return finished_columns.reshape(req_count, new_count, column_count)


def one_hot(flag):
    return jnp.where(flag, 1.0, 0.0).astype(jnp.bfloat16)


def iota(shape, axis):
    return lax.broadcasted_iota(jnp.int32, shape, axis)


def quot(values, size):
    return lax.shift_right_logical(values, size.bit_length() - 1)


def rest(values, size):
    return values & (size - 1)


def head_vectors(sums, gain, cosine, sine):
    scale = lax.rsqrt(jnp.mean(sums * sums, axis=-1, keepdims=True) + norm_eps)
    normed = sums * scale * gain
    turned = normed * cosine + pltpu.roll(normed, sums.shape[1] // 2, 1) * sine
    return turned.astype(jnp.bfloat16)


def attend(scores, allowed):
    top = jnp.max(jnp.where(allowed, scores, masked_fill), axis=-1, keepdims=True)
    weights = jnp.where(allowed, jnp.exp(scores - top), 0.0)
    return top, jnp.sum(weights, axis=-1, keepdims=True), weights.astype(jnp.bfloat16)


def store_part(ref, at, top, total, weighted):
    rows, lanes = weighted.shape
    ref[at, :rows, :] = weighted
    spread = iota((rows, lanes), 1) - iota((rows, lanes), 0)
    stats = jnp.where(spread == 0, top, 0.0) + jnp.where(spread == rows, total, 0.0)
    ref[at, pl.ds(rows, 1), :] = jnp.sum(stats, axis=0, keepdims=True)


def block_kernel(
    new_count, per_group,
    lens_hbm, sinks_hbm, freq_hbm, hidden_hbm, gain_hbm, qg_hbm, kg_hbm, wg_hbm,
    wq_hbm, wk_hbm, wv_hbm, wo_hbm, kc_hbm, vc_hbm,
    out_ref,
    lens_ref, sinks_ref, freq_ref, hidden_ref, gain_ref, qg_ref, kg_ref, wg_ref,
    wq_ref, wk_ref, wv_ref, wo_ref, kc_ref, vc_ref, placed_ref,
    part_ref, got, core_out, core_in, reduced, spread_in, summed, summed_in,
    sems, s_send, s_recv, c_send, c_recv, f_send, f_recv,
):
    loads = {}
    for n, (name, a, b) in enumerate(
        (
            ("hidden", hidden_hbm, hidden_ref), ("gain", gain_hbm, gain_ref),
            ("lens", lens_hbm, lens_ref), ("freq", freq_hbm, freq_ref),
            ("qg", qg_hbm, qg_ref), ("q", wq_hbm, wq_ref),
            ("sinks", sinks_hbm, sinks_ref), ("kc", kc_hbm, kc_ref), ("vc", vc_hbm, vc_ref),
            ("kg", kg_hbm, kg_ref), ("k", wk_hbm, wk_ref), ("v", wv_hbm, wv_ref),
            ("wg", wg_hbm, wg_ref), ("o", wo_hbm, wo_ref),
        )
    ):
        loads[name] = pltpu.make_async_copy(a, b, sems.at[n])
        loads[name].start()
    rank = lax.axis_index("seq")
    t = lax.axis_index("tp")
    z, y = rank // 2, rank % 2
    x, core = t // 2, t % 2
    crosses = core != y

    near = ((0, 1), (1, 0), (3, 0), (1, 1), (3, 1), (2, 0), (2, 1))
    wide = tuple((dz, dx) for dz in (2, 1, 3, 0) for dx in (1, 0))

    def seq_peer(dz, dy):
        return (z + dz) % 4 * 2 + (y + dy) % 2

    def spread_peer(dz, dx):
        return (z + dz) % 4 * 2 + core, (x + dx) % 2 * 2 + y

    barrier = pltpu.get_barrier_semaphore()

    def greet(seq, tp):
        pl.semaphore_signal(
            barrier, inc=1, device_id={"seq": seq, "tp": tp},
            device_id_type=pl.DeviceIdType.MESH,
        )

    for dz, dy in near:
        greet(seq_peer(dz, dy), t)
    greet(rank, x * 2 + 1 - core)
    for dz, dx in wide[:-1]:
        greet(*spread_peer(dz, dx))

    @pl.when(crosses)
    def _():
        greet(*spread_peer(0, 0))

    def remote(src, dst, send, recv, seq, tp):
        return pltpu.make_async_remote_copy(
            src_ref=src, dst_ref=dst, send_sem=send, recv_sem=recv,
            device_id={"seq": seq, "tp": tp}, device_id_type=pl.DeviceIdType.MESH,
        )

    reqs, slots, width = kc_ref.shape
    rows = reqs * new_count
    hd = freq_ref.shape[1]
    kv_heads = width // hd
    heads = kv_heads * per_group
    each = heads * new_count
    full = reqs * each
    own_reqs = reqs // 8
    own = own_reqs * each
    own_rows = own_reqs * new_count
    window = slots * 8 // 2

    loads["hidden"].wait()
    loads["gain"].wait()
    hidden = hidden_ref[...].astype(jnp.float32).reshape(rows, hidden_ref.shape[2])
    normed = (
        hidden
        * lax.rsqrt(jnp.mean(hidden * hidden, axis=1, keepdims=True) + norm_eps)
        * gain_ref[...].astype(jnp.float32).reshape(1, -1)
    ).astype(jnp.bfloat16)
    loads["lens"].wait()
    loads["freq"].wait()
    loads["qg"].wait()
    lens = lens_ref[...].astype(jnp.float32)

    def per_row(values, count, size, base):
        chosen = base + quot(iota((count, reqs), 0), size) == iota((count, reqs), 1)
        return jnp.sum(jnp.where(chosen, values, 0.0), axis=1, keepdims=True)

    token = rest(iota((rows, 1), 0), new_count).astype(jnp.float32)
    place = per_row(lens, rows, new_count, 0) + token
    low = iota((rows // 2, hd), 1) < hd // 2
    angle = jnp.where(low, place[: rows // 2], place[rows // 2 :]) * freq_ref[...]

    def unpack(packed, sign):
        turned = pltpu.roll(packed, hd // 2, 1)
        first = jnp.where(low, sign * packed, turned)
        second = jnp.where(low, sign * turned, packed)
        return jnp.concatenate([first, second], axis=0)

    cosine = unpack(jnp.cos(angle), 1.0)
    sine = unpack(jnp.sin(angle), -1.0)
    q_gain = qg_ref[...].astype(jnp.float32)

    loads["q"].wait()
    q_sum = jnp.dot(normed, wq_ref[...], preferred_element_type=jnp.float32)
    query = [
        head_vectors(q_sum[:, h * hd : (h + 1) * hd], q_gain, cosine, sine) for h in range(heads)
    ]
    at = iota((full, rows), 0)
    source = quot(at, each) * new_count + rest(at, new_count)
    hit = source == iota((full, rows), 1)
    head_of = rest(quot(at, new_count), heads)
    for k in range(kv_heads):
        picks = [one_hot(hit & (head_of == k * per_group + g)) for g in range(per_group)]
        moved = jnp.dot(
            jnp.concatenate(picks, axis=1),
            jnp.concatenate(query[k * per_group : (k + 1) * per_group], axis=0),
            preferred_element_type=jnp.float32,
        )
        placed_ref[:, k * hd : (k + 1) * hd] = moved.astype(jnp.bfloat16)

    loads["sinks"].wait()
    sinks = sinks_ref[...].astype(jnp.float32)
    loads["kc"].wait()
    loads["vc"].wait()
    contract = (((1,), (1,)), ((), ()))
    group = each // kv_heads
    pos = rank * slots + iota((own, slots), 1)

    def piece(owner):
        first = owner * own_reqs
        queries = placed_ref[pl.ds(pl.multiple_of(owner * own, own), own), :]
        scores = [
            lax.dot_general(
                queries[r * each : (r + 1) * each],
                kc_ref[first + r],
                contract,
                preferred_element_type=jnp.float32,
            )
            for r in range(own_reqs)
        ]
        scores = jnp.concatenate(scores, axis=0) * hd ** (-0.5)
        length = per_row(lens, own, each, first).astype(jnp.int32)
        sink = per_row(sinks, own, each, first).astype(jnp.int32)
        newest = length + rest(iota((own, 1), 0), new_count)
        allowed = (pos < length) & ((pos < sink) | (newest - pos < window))
        top, total, probs = attend(scores, allowed)
        weighted = []
        for r in range(own_reqs):
            both = jnp.dot(
                probs[r * each : (r + 1) * each],
                vc_ref[first + r],
                preferred_element_type=jnp.float32,
            )
            for k in range(kv_heads):
                weighted.append(both[k * group : (k + 1) * group, k * hd : (k + 1) * hd])
        return top, total, jnp.concatenate(weighted, axis=0)

    order = near + ((0, 0),)
    swaps = []
    for first in range(0, 8, 2):
        chosen = range(first, first + 2)
        results = [piece(seq_peer(*order[i])) for i in chosen]
        for i, result in zip(chosen, results):
            store_part(part_ref, i, *result)
        if first == 0:
            pl.semaphore_wait(barrier, 15 + crosses.astype(jnp.int32))
        for i in chosen:
            if i < 7:
                copy = remote(
                    part_ref.at[i], got.at[i], s_send.at[i], s_recv.at[i],
                    seq_peer(*order[i]), t,
                )
                copy.start()
                swaps.append(copy)

    loads["kg"].wait()
    k_gain = kg_ref[...].astype(jnp.float32)
    loads["k"].wait()
    k_sum = jnp.dot(normed, wk_ref[...], preferred_element_type=jnp.float32)
    keys = jnp.concatenate(
        [
            head_vectors(k_sum[:, k * hd : (k + 1) * hd], k_gain, cosine, sine)
            for k in range(kv_heads)
        ],
        axis=1,
    )
    loads["v"].wait()
    values = jnp.dot(normed, wv_ref[...], preferred_element_type=jnp.float32).astype(jnp.bfloat16)
    mine = placed_ref[pl.ds(pl.multiple_of(rank * own, own), own), :]
    fresh = lax.dot_general(mine, keys, contract, preferred_element_type=jnp.float32)
    fresh = fresh * hd ** (-0.5)
    row = iota((own, rows), 0)
    col = iota((own, rows), 1)
    own_req = rank * own_reqs + quot(row, each)
    visible = (quot(col, new_count) == own_req) & (rest(col, new_count) <= rest(row, new_count))
    top, total, probs = attend(fresh, visible)
    both = jnp.dot(probs, values, preferred_element_type=jnp.float32)
    row_head = rest(quot(iota((own, hd), 0), new_count), heads)
    picked = jnp.zeros((own, hd), jnp.float32)
    for k in range(kv_heads):
        picked = jnp.where(quot(row_head, per_group) == k, both[:, k * hd : (k + 1) * hd], picked)
    store_part(part_ref, 8, top, total, picked)

    loads["wg"].wait()
    logits = lax.dot_general(normed, wg_ref[...], contract, preferred_element_type=jnp.float32)
    gates = jax.nn.sigmoid(logits).astype(jnp.bfloat16)
    pick = one_hot(col == own_req * new_count + rest(row, new_count))
    gates = jnp.dot(pick, gates, preferred_element_type=jnp.float32)
    small = (own, heads)
    gates = jnp.where(rest(quot(iota(small, 0), new_count), heads) == iota(small, 1), gates, 0.0)
    gate = jnp.sum(gates, axis=1, keepdims=True)

    row = iota((own_rows, own), 0)
    col = iota((own_rows, own), 1)
    base = quot(row, new_count) * each + rest(row, new_count)
    back = [one_hot(col == base + h * new_count) for h in range(heads)]
    loads["o"].wait()

    pieces = [part_ref[7], part_ref[8]]
    for i, copy in enumerate(swaps):
        copy.wait_recv()
        pieces.append(got[i])
    stats = [p[own : own + 1, :] for p in pieces]
    top = functools.reduce(jnp.maximum, stats)
    scales = [jnp.exp(jnp.minimum(p - top, 0.0)) for p in stats]
    total = functools.reduce(
        jnp.add, [pltpu.roll(p, own, 1) * scale for p, scale in zip(stats, scales)]
    )
    diagonal = iota((own, hd), 1) == iota((own, hd), 0)
    weighted = jnp.zeros((own, hd), jnp.float32)
    for p, scale in zip(pieces, scales):
        share = jnp.sum(jnp.where(diagonal, scale / total, 0.0), axis=1, keepdims=True)
        weighted = weighted + p[:own, :] * share
    gated = (weighted * gate).astype(jnp.bfloat16)
    lined = jnp.concatenate(
        [
            jnp.dot(b, gated, preferred_element_type=jnp.float32).astype(jnp.bfloat16)
            for b in back
        ],
        axis=1,
    )
    cols = out_ref.shape[2]

    def project(j, parity):
        start = pl.multiple_of((2 * j + parity) * cols, cols)
        return jnp.dot(lined, wo_ref[:, pl.ds(start, cols)], preferred_element_type=jnp.float32)

    for j in range(4):
        core_out[j] = project(j, 1 - core)
    to_core = remote(
        core_out, core_in, c_send.at[0], c_recv.at[0], rank, x * 2 + 1 - core
    )
    to_core.start()
    for j in range(4):
        reduced[j] = project(j, core)
    to_core.wait_recv()
    for j in range(4):
        reduced[j] = reduced[j] + core_in[j]

    spreads = []
    for n, (dz, dx) in enumerate(wide):
        copy = remote(
            reduced.at[(z + dz) % 4], spread_in.at[dz, dx], f_send.at[n], f_recv.at[n],
            *spread_peer(dz, dx),
        )
        spreads.append(copy)
        if n < 7:
            copy.start()
        else:

            @pl.when(crosses)
            def _():
                copy.start()

            @pl.when(jnp.logical_not(crosses))
            def _():
                spread_in[0, 0] = reduced[z]

    column = pl.multiple_of(rank * cols, cols)

    def finish(source_z, parity, block):
        at = pl.ds((source_z * 2 + parity) * own_reqs, own_reqs)
        residual = hidden_ref[at, :, pl.ds(column, cols)].astype(jnp.float32)
        block = block.reshape(own_reqs, new_count, cols)
        out_ref[at] = (residual + block).astype(out_ref.dtype)

    for dz in (0, 1, 3, 2):
        for n, (d, dx) in enumerate(wide):
            if d == dz:
                if n < 7:
                    spreads[n].wait_recv()
                else:

                    @pl.when(crosses)
                    def _():
                        spreads[7].wait_recv()

        summed[(z - dz + 4) % 4] = spread_in[dz, 0] + spread_in[dz, 1]
    back_core = remote(
        summed, summed_in, c_send.at[1], c_recv.at[1], rank, x * 2 + 1 - core
    )
    back_core.start()
    for k in range(4):
        finish(k, core, summed[k])
    back_core.wait_recv()
    for k in range(4):
        finish(k, 1 - core, summed_in[k])

    for copy in swaps + [to_core, back_core] + spreads[:7]:
        copy.wait_send()

    @pl.when(crosses)
    def _():
        spreads[7].wait_send()


def fits(seq_count, tp_count, reqs, new_count, heads, slots, hd, model_width):
    own = reqs // seq_count * heads * new_count
    return (
        seq_count == 8
        and tp_count == 4
        and reqs % seq_count == 0
        and model_width % (128 * seq_count) == 0
        and own % 16 == 0
        and 2 * own == hd == slots == 128
        and reqs * new_count == 128
        and heads & (heads - 1) == 0
    )


def per_device(
    hidden_in, key_cache, value_cache, cache_len, sink_count, attn_gain,
    w_query, w_key, w_value, w_headgate, q_gain, k_gain, w_output,
):
    reqs, new_count, model_width = hidden_in.shape
    hd = q_gain.shape[0]
    slots, width = key_cache.shape[1:]
    seq_count = lax.axis_size("seq")
    tp_count = lax.axis_size("tp")
    heads = w_query.shape[1] // hd
    if not fits(seq_count, tp_count, reqs, new_count, heads, slots, hd, model_width):
        return plain_device(
            hidden_in, key_cache, value_cache, cache_len, sink_count, attn_gain,
            w_query, w_key, w_value, w_headgate, q_gain, k_gain, w_output,
        )
    each = heads * new_count
    own = reqs // seq_count * each
    freq = np.tile(rope_theta ** (-np.arange(hd // 2) * 2.0 / hd), 2)[None, :].astype(np.float32)
    f32 = jnp.float32
    own_rows = own // heads
    cols = model_width // seq_count
    sem = pltpu.SemaphoreType.DMA
    operands = (
        cache_len[None, :], sink_count[None, :], freq, hidden_in, attn_gain,
        q_gain[None, :], k_gain[None, :], w_headgate.T,
        w_query, w_key, w_value, w_output, key_cache, value_cache,
    )
    return pl.pallas_call(
        functools.partial(block_kernel, new_count, heads * hd // width),
        out_shape=pltpu.VMEM((reqs, new_count, cols), hidden_in.dtype),
        in_specs=[pl.BlockSpec(memory_space=pl.ANY)] * len(operands),
        out_specs=pl.BlockSpec(memory_space=pltpu.VMEM),
        scratch_shapes=[pltpu.VMEM(a.shape, a.dtype) for a in operands]
        + [
            pltpu.VMEM((reqs * each, width), jnp.bfloat16),
            pltpu.VMEM((9, own + 1, hd), f32),
            pltpu.VMEM((7, own + 1, hd), f32),
            pltpu.VMEM((4, own_rows, cols), f32),
            pltpu.VMEM((4, own_rows, cols), f32),
            pltpu.VMEM((4, own_rows, cols), f32),
            pltpu.VMEM((4, 2, own_rows, cols), f32),
            pltpu.VMEM((4, own_rows, cols), f32),
            pltpu.VMEM((4, own_rows, cols), f32),
            sem((len(operands),)),
            sem((7,)), sem((7,)), sem((2,)), sem((2,)), sem((8,)), sem((8,)),
        ],
        compiler_params=pltpu.CompilerParams(collective_id=0, has_side_effects=True),
        name="attention_block",
    )(*operands)


def solution(mesh):
    placed = (
        P(),
        P(None, "seq", "tp"),
        P(None, "seq", "tp"),
        P(),
        P(),
        P(),
        P(None, "tp"),
        P(None, "tp"),
        P(None, "tp"),
        P(None, "tp"),
        P(),
        P(),
        P("tp", None),
    )
    return jax.shard_map(
        per_device, mesh=mesh, in_specs=placed, out_specs=P(None, None, "seq"), check_vma=False
    )
```

```python
import functools

import jax
import jax.numpy as jnp
import numpy as np
from jax import lax
from jax.experimental import pallas as pl
from jax.experimental.pallas import tpu as pltpu
from jax.sharding import PartitionSpec as P

rope_theta = 1000000.0
norm_eps = 1e-06
masked_fill = -1e30


def rms_scale(values, gain_vec):
    mean_sq = jnp.mean(values * values, axis=-1, keepdims=True)
    return values * lax.rsqrt(mean_sq + norm_eps) * gain_vec.astype(jnp.float32)


def rotate(values, positions):
    half_dim = values.shape[-1] // 2
    inv_freq = rope_theta ** (-jnp.arange(half_dim, dtype=jnp.float32) * 2.0 / values.shape[-1])
    phases = positions.astype(jnp.float32)[:, None] * inv_freq[None, :]
    cosine = jnp.cos(phases)[:, None, :]
    sine_term = jnp.sin(phases)[:, None, :]
    lower_half = values[..., :half_dim]
    upper_half = values[..., half_dim:]
    return jnp.concatenate(
        [
            lower_half * cosine - upper_half * sine_term,
            upper_half * cosine + lower_half * sine_term,
        ],
        axis=-1,
    )


def finish_heads(query, new_keys, new_values, gate_logit, positions, q_gain, k_gain):
    row_count = query.shape[0]
    head_dim = q_gain.shape[0]
    query_heads = rotate(rms_scale(query.reshape(row_count, -1, head_dim), q_gain), positions)
    key_heads = rotate(rms_scale(new_keys.reshape(row_count, -1, head_dim), k_gain), positions)
    return (
        query_heads.reshape(row_count, -1).astype(jnp.bfloat16),
        key_heads.reshape(row_count, -1).astype(jnp.bfloat16),
        new_values.astype(jnp.bfloat16),
        jax.nn.sigmoid(gate_logit).astype(jnp.bfloat16),
    )


def softmax_part(scores, allowed, value_rows, form):
    top_score = jnp.max(jnp.where(allowed, scores, masked_fill), axis=-1)
    weights = jnp.where(allowed, jnp.exp(scores - top_score[..., None]), 0.0)
    weight_sum = jnp.sum(weights, axis=-1)
    weighted = jnp.einsum(
        form, weights.astype(jnp.bfloat16), value_rows, preferred_element_type=jnp.float32
    )
    return (top_score, weight_sum, weighted)


def join_parts(first_part, second_part):
    top_score = jnp.maximum(first_part[0], second_part[0])
    left_scale = jnp.exp(first_part[0] - top_score)
    right_scale = jnp.exp(second_part[0] - top_score)
    return (
        top_score,
        first_part[1] * left_scale + second_part[1] * right_scale,
        first_part[2] * left_scale[..., None] + second_part[2] * right_scale[..., None],
    )


def piece_attention(queries, cache_keys, cache_values, lengths, sinks, offset, window):
    req_count, slot_count = (cache_keys.shape[0], cache_keys.shape[1])
    kv_heads, head_dim = (queries.shape[2], queries.shape[4])
    key_rows = cache_keys.reshape(req_count, slot_count, kv_heads, head_dim)
    value_rows = cache_values.reshape(req_count, slot_count, kv_heads, head_dim)
    scores = jnp.einsum(
        "rtkgd,rskd->rkgts", queries, key_rows, preferred_element_type=jnp.float32
    ) * head_dim ** (-0.5)
    cache_pos = offset + jnp.arange(slot_count, dtype=jnp.int32)
    newest_pos = lengths[:, None] + jnp.arange(queries.shape[1], dtype=jnp.int32)[None, :]
    allowed = (cache_pos[None, None, :] < lengths[:, None, None]) & (
        (cache_pos[None, None, :] < sinks[:, None, None])
        | (newest_pos[:, :, None] - cache_pos[None, None, :] < window)
    )
    return softmax_part(scores, allowed[:, None, None, :, :], value_rows, "rkgts,rskd->rkgtd")


def plain_device(
    hidden_in,
    key_cache,
    value_cache,
    cache_len,
    sink_count,
    attn_gain,
    w_query,
    w_key,
    w_value,
    w_headgate,
    q_gain,
    k_gain,
    w_output,
):
    req_count, new_count, model_width = hidden_in.shape
    head_dim = q_gain.shape[0]
    seq_count = lax.axis_size("seq")
    seq_rank = lax.axis_index("seq")
    row_count = req_count * new_count
    window = key_cache.shape[1] * seq_count // 2
    residual = hidden_in.reshape(row_count, model_width).astype(jnp.float32)
    normed = (
        residual
        * lax.rsqrt(jnp.mean(residual * residual, axis=1) + norm_eps)[:, None]
        * attn_gain.astype(jnp.float32)
    ).astype(jnp.bfloat16)
    positions = (cache_len[:, None] + jnp.arange(new_count, dtype=jnp.int32)[None, :]).reshape(
        row_count
    )
    query, new_keys, new_values, head_gate = finish_heads(
        jnp.dot(normed, w_query, preferred_element_type=jnp.float32),
        jnp.dot(normed, w_key, preferred_element_type=jnp.float32),
        jnp.dot(normed, w_value, preferred_element_type=jnp.float32),
        jnp.dot(normed, w_headgate, preferred_element_type=jnp.float32),
        positions,
        q_gain,
        k_gain,
    )
    kv_local = new_keys.shape[1] // head_dim
    q_local = query.shape[1] // head_dim
    per_group = q_local // kv_local
    query_grid = query.reshape(req_count, new_count, kv_local, per_group, head_dim)
    offset = seq_rank * key_cache.shape[1]
    cache_part = piece_attention(
        query_grid, key_cache, value_cache, cache_len, sink_count, offset, window
    )
    top_score = lax.pmax(cache_part[0], "seq")
    rescale = jnp.exp(cache_part[0] - top_score)
    weight_sum, weighted = lax.psum(
        (cache_part[1] * rescale, cache_part[2] * rescale[..., None]), "seq"
    )
    key_grid = new_keys.reshape(req_count, new_count, kv_local, head_dim)
    value_grid = new_values.reshape(req_count, new_count, kv_local, head_dim)
    fresh_scores = jnp.einsum(
        "rtkgd,rjkd->rkgtj", query_grid, key_grid, preferred_element_type=jnp.float32
    ) * head_dim ** (-0.5)
    causal_mask = (
        jnp.arange(new_count, dtype=jnp.int32)[None, :]
        <= jnp.arange(new_count, dtype=jnp.int32)[:, None]
    )
    fresh_part = softmax_part(
        fresh_scores, causal_mask[None, None, None, :, :], value_grid, "rkgtj,rjkd->rkgtd"
    )
    top_score, weight_sum, weighted = join_parts((top_score, weight_sum, weighted), fresh_part)
    attended = weighted / weight_sum[..., None]
    attended = jnp.transpose(attended, (0, 3, 1, 2, 4)).reshape(row_count, q_local, head_dim)
    gated = (
        (attended * head_gate.astype(jnp.float32)[:, :, None])
        .astype(jnp.bfloat16)
        .reshape(row_count, q_local * head_dim)
    )
    column_count = model_width // seq_count
    column_start = seq_rank * column_count
    residual_columns = lax.dynamic_slice_in_dim(residual, column_start, column_count, 1)
    projected = lax.psum(jnp.dot(gated, w_output, preferred_element_type=jnp.float32), "tp")
    projected_columns = lax.dynamic_slice_in_dim(projected, column_start, column_count, 1)
    finished_columns = (residual_columns + projected_columns).astype(jnp.bfloat16)
    return finished_columns.reshape(req_count, new_count, column_count)


def one_hot(flag):
    return jnp.where(flag, 1.0, 0.0).astype(jnp.bfloat16)


def iota(shape, axis):
    return lax.broadcasted_iota(jnp.int32, shape, axis)


def quot(values, size):
    return lax.shift_right_logical(values, size.bit_length() - 1)


def rest(values, size):
    return values & (size - 1)


def head_vectors(sums, gain, cosine, sine):
    scale = lax.rsqrt(jnp.mean(sums * sums, axis=-1, keepdims=True) + norm_eps)
    normed = sums * scale * gain
    turned = normed * cosine + pltpu.roll(normed, sums.shape[1] // 2, 1) * sine
    return turned.astype(jnp.bfloat16)


def attend(scores, allowed):
    top = jnp.max(jnp.where(allowed, scores, masked_fill), axis=-1, keepdims=True)
    weights = jnp.where(allowed, jnp.exp(scores - top), 0.0)
    return top, jnp.sum(weights, axis=-1, keepdims=True), weights.astype(jnp.bfloat16)


def store_part(ref, at, top, total, weighted):
    rows, lanes = weighted.shape
    ref[at, :rows, :] = weighted
    spread = iota((rows, lanes), 1) - iota((rows, lanes), 0)
    stats = jnp.where(spread == 0, top, 0.0) + jnp.where(spread == rows, total, 0.0)
    ref[at, pl.ds(rows, 1), :] = jnp.sum(stats, axis=0, keepdims=True)


def block_kernel(
    new_count, per_group,
    lens_hbm, sinks_hbm, freq_hbm, hidden_hbm, gain_hbm, qg_hbm, kg_hbm, wg_hbm,
    wq_hbm, wk_hbm, wv_hbm, wo_hbm, kc_hbm, vc_hbm,
    out_ref,
    lens_ref, sinks_ref, freq_ref, hidden_ref, gain_ref, qg_ref, kg_ref, wg_ref,
    wq_ref, wk_ref, wv_ref, wo_ref, kc_ref, vc_ref, placed_ref,
    part_ref, got, core_out, core_in, reduced, spread_in, summed, summed_in,
    sems, s_send, s_recv, c_send, c_recv, f_send, f_recv,
):
    rank = lax.axis_index("seq")
    t = lax.axis_index("tp")
    z, y = rank // 2, rank % 2
    x, core = t // 2, t % 2
    crosses = core != y

    near = ((2, 1), (2, 0), (3, 1), (3, 0), (1, 1), (1, 0), (0, 1))
    wide = tuple((dz, dx) for dz in (3, 2, 1, 0) for dx in (1, 0))

    def seq_peer(dz, dy):
        return (z ^ dz) * 2 + (y ^ dy)

    def spread_peer(dz, dx):
        return (z ^ dz) * 2 + core, (x ^ dx) * 2 + y

    barrier = pltpu.get_barrier_semaphore()

    def greet(seq, tp):
        pl.semaphore_signal(
            barrier, inc=1, device_id={"seq": seq, "tp": tp},
            device_id_type=pl.DeviceIdType.MESH,
        )

    for dz, dy in near:
        greet(seq_peer(dz, dy), t)
    for i in (2, 3, 1):
        greet(rank, t ^ i)

    loads = {}
    for n, (name, a, b) in enumerate(
        (
            ("hidden", hidden_hbm, hidden_ref), ("gain", gain_hbm, gain_ref),
            ("lens", lens_hbm, lens_ref), ("freq", freq_hbm, freq_ref),
            ("qg", qg_hbm, qg_ref), ("q", wq_hbm, wq_ref),
            ("sinks", sinks_hbm, sinks_ref), ("kc", kc_hbm, kc_ref), ("vc", vc_hbm, vc_ref),
            ("kg", kg_hbm, kg_ref), ("k", wk_hbm, wk_ref), ("v", wv_hbm, wv_ref),
            ("wg", wg_hbm, wg_ref), ("o", wo_hbm, wo_ref),
        )
    ):
        loads[name] = pltpu.make_async_copy(a, b, sems.at[n])
        loads[name].start()

    def remote(src, dst, send, recv, seq, tp):
        return pltpu.make_async_remote_copy(
            src_ref=src, dst_ref=dst, send_sem=send, recv_sem=recv,
            device_id={"seq": seq, "tp": tp}, device_id_type=pl.DeviceIdType.MESH,
        )

    reqs, slots, width = kc_ref.shape
    rows = reqs * new_count
    hd = freq_ref.shape[1]
    kv_heads = width // hd
    heads = kv_heads * per_group
    each = heads * new_count
    full = reqs * each
    own_reqs = reqs // 8
    own = own_reqs * each
    own_rows = own_reqs * new_count
    window = slots * 8 // 2

    loads["hidden"].wait()
    loads["gain"].wait()
    hidden = hidden_ref[...].astype(jnp.float32).reshape(rows, hidden_ref.shape[2])
    normed = (
        hidden
        * lax.rsqrt(jnp.mean(hidden * hidden, axis=1, keepdims=True) + norm_eps)
        * gain_ref[...].astype(jnp.float32).reshape(1, -1)
    ).astype(jnp.bfloat16)
    loads["lens"].wait()
    loads["freq"].wait()
    loads["qg"].wait()
    lens = lens_ref[...].astype(jnp.float32)

    def per_row(values, count, size, base):
        chosen = base + quot(iota((count, reqs), 0), size) == iota((count, reqs), 1)
        return jnp.sum(jnp.where(chosen, values, 0.0), axis=1, keepdims=True)

    token = rest(iota((rows, 1), 0), new_count).astype(jnp.float32)
    place = per_row(lens, rows, new_count, 0) + token
    low = iota((rows // 2, hd), 1) < hd // 2
    angle = jnp.where(low, place[: rows // 2], place[rows // 2 :]) * freq_ref[...]

    def unpack(packed, sign):
        turned = pltpu.roll(packed, hd // 2, 1)
        first = jnp.where(low, sign * packed, turned)
        second = jnp.where(low, sign * turned, packed)
        return jnp.concatenate([first, second], axis=0)

    cosine = unpack(jnp.cos(angle), 1.0)
    sine = unpack(jnp.sin(angle), -1.0)
    q_gain = qg_ref[...].astype(jnp.float32)

    loads["q"].wait()
    q_sum = jnp.dot(normed, wq_ref[...], preferred_element_type=jnp.float32)
    query = [
        head_vectors(q_sum[:, h * hd : (h + 1) * hd], q_gain, cosine, sine) for h in range(heads)
    ]
    at = iota((full, rows), 0)
    source = quot(at, each) * new_count + rest(at, new_count)
    hit = source == iota((full, rows), 1)
    head_of = rest(quot(at, new_count), heads)
    for k in range(kv_heads):
        picks = [one_hot(hit & (head_of == k * per_group + g)) for g in range(per_group)]
        moved = jnp.dot(
            jnp.concatenate(picks, axis=1),
            jnp.concatenate(query[k * per_group : (k + 1) * per_group], axis=0),
            preferred_element_type=jnp.float32,
        )
        placed_ref[:, k * hd : (k + 1) * hd] = moved.astype(jnp.bfloat16)

    loads["sinks"].wait()
    sinks = sinks_ref[...].astype(jnp.float32)
    loads["kc"].wait()
    loads["vc"].wait()
    contract = (((1,), (1,)), ((), ()))
    group = each // kv_heads
    pos = rank * slots + iota((own, slots), 1)

    def piece(owner):
        first = owner * own_reqs
        queries = placed_ref[pl.ds(pl.multiple_of(owner * own, own), own), :]
        scores = [
            lax.dot_general(
                queries[r * each : (r + 1) * each],
                kc_ref[first + r],
                contract,
                preferred_element_type=jnp.float32,
            )
            for r in range(own_reqs)
        ]
        scores = jnp.concatenate(scores, axis=0) * hd ** (-0.5)
        length = per_row(lens, own, each, first).astype(jnp.int32)
        sink = per_row(sinks, own, each, first).astype(jnp.int32)
        newest = length + rest(iota((own, 1), 0), new_count)
        allowed = (pos < length) & ((pos < sink) | (newest - pos < window))
        top, total, probs = attend(scores, allowed)
        weighted = []
        for r in range(own_reqs):
            both = jnp.dot(
                probs[r * each : (r + 1) * each],
                vc_ref[first + r],
                preferred_element_type=jnp.float32,
            )
            for k in range(kv_heads):
                weighted.append(both[k * group : (k + 1) * group, k * hd : (k + 1) * hd])
        return top, total, jnp.concatenate(weighted, axis=0)

    order = near + ((0, 0),)
    passed, joined = order.index((2, 1)), order.index((2, 0))
    swaps = []
    for first in range(0, 8, 2):
        chosen = range(first, first + 2)
        results = [piece(seq_peer(*order[i])) for i in chosen]
        for i, result in zip(chosen, results):
            store_part(part_ref, i, *result)
        if first == 0:
            pl.semaphore_wait(barrier, 10)
        for i in chosen:
            if i < 7:
                copy = remote(
                    part_ref.at[9 if i == joined else i], got.at[i], s_send.at[i], s_recv.at[i],
                    seq_peer(0, 1) if i == passed else seq_peer(*order[i]), t,
                )
                if i != joined:
                    copy.start()
                swaps.append(copy)

    def join(parts):
        stats = [p[own : own + 1, :] for p in parts]
        top = functools.reduce(jnp.maximum, stats)
        scales = [jnp.exp(jnp.minimum(p - top, 0.0)) for p in stats]
        total = functools.reduce(
            jnp.add, [pltpu.roll(p, own, 1) * scale for p, scale in zip(stats, scales)]
        )
        return top, scales, total

    diagonal = iota((own, hd), 1) == iota((own, hd), 0)

    def column(line):
        return jnp.sum(jnp.where(diagonal, line, 0.0), axis=1, keepdims=True)

    def send_joined():
        swaps[passed].wait_recv()
        parts = [part_ref[joined], got[passed]]
        top, scales, total = join(parts)
        part_ref[9, :own, :] = parts[0][:own, :] * column(scales[0]) + parts[1][:own, :] * column(scales[1])
        lanes = iota((1, hd), 1)
        part_ref[9, pl.ds(own, 1), :] = jnp.where(lanes < own, top, pltpu.roll(total, own, 1))
        swaps[joined].start()

    loads["kg"].wait()
    k_gain = kg_ref[...].astype(jnp.float32)
    loads["k"].wait()
    k_sum = jnp.dot(normed, wk_ref[...], preferred_element_type=jnp.float32)
    keys = jnp.concatenate(
        [
            head_vectors(k_sum[:, k * hd : (k + 1) * hd], k_gain, cosine, sine)
            for k in range(kv_heads)
        ],
        axis=1,
    )
    loads["v"].wait()
    values = jnp.dot(normed, wv_ref[...], preferred_element_type=jnp.float32).astype(jnp.bfloat16)
    mine = placed_ref[pl.ds(pl.multiple_of(rank * own, own), own), :]
    fresh = lax.dot_general(mine, keys, contract, preferred_element_type=jnp.float32)
    fresh = fresh * hd ** (-0.5)
    row = iota((own, rows), 0)
    col = iota((own, rows), 1)
    own_req = rank * own_reqs + quot(row, each)
    visible = (quot(col, new_count) == own_req) & (rest(col, new_count) <= rest(row, new_count))
    top, total, probs = attend(fresh, visible)
    both = jnp.dot(probs, values, preferred_element_type=jnp.float32)
    row_head = rest(quot(iota((own, hd), 0), new_count), heads)
    picked = jnp.zeros((own, hd), jnp.float32)
    for k in range(kv_heads):
        picked = jnp.where(quot(row_head, per_group) == k, both[:, k * hd : (k + 1) * hd], picked)
    store_part(part_ref, 8, top, total, picked)

    send_joined()
    loads["wg"].wait()
    logits = lax.dot_general(normed, wg_ref[...], contract, preferred_element_type=jnp.float32)
    gates = jax.nn.sigmoid(logits).astype(jnp.bfloat16)
    pick = one_hot(col == own_req * new_count + rest(row, new_count))
    gates = jnp.dot(pick, gates, preferred_element_type=jnp.float32)
    small = (own, heads)
    gates = jnp.where(rest(quot(iota(small, 0), new_count), heads) == iota(small, 1), gates, 0.0)
    gate = jnp.sum(gates, axis=1, keepdims=True)

    row = iota((own_rows, own), 0)
    col = iota((own_rows, own), 1)
    base = quot(row, new_count) * each + rest(row, new_count)
    back = [one_hot(col == base + h * new_count) for h in range(heads)]
    loads["o"].wait()

    pieces = [part_ref[7], part_ref[8]]
    for i, copy in enumerate(swaps):
        if i != passed:
            copy.wait_recv()
            pieces.append(got[i])
    top, scales, total = join(pieces)
    weighted = jnp.zeros((own, hd), jnp.float32)
    for p, scale in zip(pieces, scales):
        weighted = weighted + p[:own, :] * column(scale / total)
    gated = (weighted * gate).astype(jnp.bfloat16)
    lined = jnp.concatenate(
        [
            jnp.dot(b, gated, preferred_element_type=jnp.float32).astype(jnp.bfloat16)
            for b in back
        ],
        axis=1,
    )
    cols = out_ref.shape[2]

    def project(j, parity):
        start = pl.multiple_of((2 * j + parity) * cols, cols)
        return jnp.dot(lined, wo_ref[:, pl.ds(start, cols)], preferred_element_type=jnp.float32)

    far = [wide[0][0], wide[2][0], wide[4][0], wide[6][0]]
    to_core = []
    for half in range(2):
        pair = pl.ds(2 * half, 2)
        for i in (2 * half, 2 * half + 1):
            core_out[i] = project(z ^ far[i], 1 - core)
        copy = remote(
            core_out.at[pair], core_in.at[pair], c_send.at[half], c_recv.at[half], rank, t ^ 1
        )
        copy.start()
        to_core.append(copy)
    for i in range(4):
        reduced[i] = project(z ^ far[i], core)

    spreads = []
    for n, (dz, dx) in enumerate(wide):
        if n in (0, 4):
            to_core[n // 4].wait_recv()
            for i in (n // 2, n // 2 + 1):
                reduced[i] = reduced[i] + core_in[i]
        copy = remote(
            reduced.at[n // 2], spread_in.at[dz, dx], f_send.at[n], f_recv.at[n],
            *spread_peer(dz, dx),
        )
        spreads.append(copy)
        if n < 7:
            copy.start()
        else:

            @pl.when(crosses)
            def _():
                copy.start()

            @pl.when(jnp.logical_not(crosses))
            def _():
                spread_in[0, 0] = reduced[3]

    column = pl.multiple_of(rank * cols, cols)

    def finish(source_z, parity, block):
        at = pl.ds((source_z * 2 + parity) * own_reqs, own_reqs)
        residual = hidden_ref[at, :, pl.ds(column, cols)].astype(jnp.float32)
        block = block.reshape(own_reqs, new_count, cols)
        out_ref[at] = (residual + block).astype(out_ref.dtype)

    near_first = far[::-1]
    back_core = []
    for half in range(2):
        pair = pl.ds(2 * half, 2)
        for i in (2 * half, 2 * half + 1):
            for dx in (1, 0):
                n = wide.index((near_first[i], dx))
                if n < 7:
                    spreads[n].wait_recv()
                else:

                    @pl.when(crosses)
                    def _():
                        spreads[7].wait_recv()

            summed[i] = spread_in[near_first[i], 0] + spread_in[near_first[i], 1]
        copy = remote(
            summed.at[pair], summed_in.at[pair],
            c_send.at[2 + half], c_recv.at[2 + half], rank, t ^ 1,
        )
        copy.start()
        back_core.append(copy)
    for i in range(4):
        finish(z ^ near_first[i], core, summed[i])
    for half in range(2):
        back_core[half].wait_recv()
        for i in (2 * half, 2 * half + 1):
            finish(z ^ near_first[i], 1 - core, summed_in[i])

    for copy in swaps + to_core + back_core + spreads[:7]:
        copy.wait_send()

    @pl.when(crosses)
    def _():
        spreads[7].wait_send()


def fits(seq_count, tp_count, reqs, new_count, heads, slots, hd, model_width):
    own = reqs // seq_count * heads * new_count
    return (
        seq_count == 8
        and tp_count == 4
        and reqs % seq_count == 0
        and model_width % (128 * seq_count) == 0
        and own % 16 == 0
        and 2 * own == hd == slots == 128
        and reqs * new_count == 128
        and heads & (heads - 1) == 0
    )


def per_device(
    hidden_in, key_cache, value_cache, cache_len, sink_count, attn_gain,
    w_query, w_key, w_value, w_headgate, q_gain, k_gain, w_output,
):
    reqs, new_count, model_width = hidden_in.shape
    hd = q_gain.shape[0]
    slots, width = key_cache.shape[1:]
    seq_count = lax.axis_size("seq")
    tp_count = lax.axis_size("tp")
    heads = w_query.shape[1] // hd
    if not fits(seq_count, tp_count, reqs, new_count, heads, slots, hd, model_width):
        return plain_device(
            hidden_in, key_cache, value_cache, cache_len, sink_count, attn_gain,
            w_query, w_key, w_value, w_headgate, q_gain, k_gain, w_output,
        )
    each = heads * new_count
    own = reqs // seq_count * each
    freq = np.tile(rope_theta ** (-np.arange(hd // 2) * 2.0 / hd), 2)[None, :].astype(np.float32)
    f32 = jnp.float32
    own_rows = own // heads
    cols = model_width // seq_count
    sem = pltpu.SemaphoreType.DMA
    operands = (
        cache_len[None, :], sink_count[None, :], freq, hidden_in, attn_gain,
        q_gain[None, :], k_gain[None, :], w_headgate.T,
        w_query, w_key, w_value, w_output, key_cache, value_cache,
    )
    return pl.pallas_call(
        functools.partial(block_kernel, new_count, heads * hd // width),
        out_shape=pltpu.VMEM((reqs, new_count, cols), hidden_in.dtype),
        in_specs=[pl.BlockSpec(memory_space=pl.ANY)] * len(operands),
        out_specs=pl.BlockSpec(memory_space=pltpu.VMEM),
        scratch_shapes=[pltpu.VMEM(a.shape, a.dtype) for a in operands]
        + [
            pltpu.VMEM((reqs * each, width), jnp.bfloat16),
            pltpu.VMEM((10, own + 1, hd), f32),
            pltpu.VMEM((7, own + 1, hd), f32),
            pltpu.VMEM((4, own_rows, cols), f32),
            pltpu.VMEM((4, own_rows, cols), f32),
            pltpu.VMEM((4, own_rows, cols), f32),
            pltpu.VMEM((4, 2, own_rows, cols), f32),
            pltpu.VMEM((4, own_rows, cols), f32),
            pltpu.VMEM((4, own_rows, cols), f32),
            sem((len(operands),)),
            sem((7,)), sem((7,)), sem((4,)), sem((4,)), sem((8,)), sem((8,)),
        ],
        compiler_params=pltpu.CompilerParams(collective_id=0, has_side_effects=True),
        name="attention_block",
    )(*operands)


def solution(mesh):
    placed = (
        P(),
        P(None, "seq", "tp"),
        P(None, "seq", "tp"),
        P(),
        P(),
        P(),
        P(None, "tp"),
        P(None, "tp"),
        P(None, "tp"),
        P(None, "tp"),
        P(),
        P(),
        P("tp", None),
    )
    return jax.shard_map(
        per_device, mesh=mesh, in_specs=placed, out_specs=P(None, None, "seq"), check_vma=False
    )
```

```python
import functools

import jax
import jax.numpy as jnp
import numpy as np
from jax import lax
from jax.experimental import pallas as pl
from jax.experimental.pallas import tpu as pltpu
from jax.sharding import PartitionSpec as P

rope_theta = 1000000.0
norm_eps = 1e-06
masked_fill = -1e30


def rms_scale(values, gain_vec):
    mean_sq = jnp.mean(values * values, axis=-1, keepdims=True)
    return values * lax.rsqrt(mean_sq + norm_eps) * gain_vec.astype(jnp.float32)


def rotate(values, positions):
    half_dim = values.shape[-1] // 2
    inv_freq = rope_theta ** (-jnp.arange(half_dim, dtype=jnp.float32) * 2.0 / values.shape[-1])
    phases = positions.astype(jnp.float32)[:, None] * inv_freq[None, :]
    cosine = jnp.cos(phases)[:, None, :]
    sine_term = jnp.sin(phases)[:, None, :]
    lower_half = values[..., :half_dim]
    upper_half = values[..., half_dim:]
    return jnp.concatenate(
        [
            lower_half * cosine - upper_half * sine_term,
            upper_half * cosine + lower_half * sine_term,
        ],
        axis=-1,
    )


def finish_heads(query, new_keys, new_values, gate_logit, positions, q_gain, k_gain):
    row_count = query.shape[0]
    head_dim = q_gain.shape[0]
    query_heads = rotate(rms_scale(query.reshape(row_count, -1, head_dim), q_gain), positions)
    key_heads = rotate(rms_scale(new_keys.reshape(row_count, -1, head_dim), k_gain), positions)
    return (
        query_heads.reshape(row_count, -1).astype(jnp.bfloat16),
        key_heads.reshape(row_count, -1).astype(jnp.bfloat16),
        new_values.astype(jnp.bfloat16),
        jax.nn.sigmoid(gate_logit).astype(jnp.bfloat16),
    )


def softmax_part(scores, allowed, value_rows, form):
    top_score = jnp.max(jnp.where(allowed, scores, masked_fill), axis=-1)
    weights = jnp.where(allowed, jnp.exp(scores - top_score[..., None]), 0.0)
    weight_sum = jnp.sum(weights, axis=-1)
    weighted = jnp.einsum(
        form, weights.astype(jnp.bfloat16), value_rows, preferred_element_type=jnp.float32
    )
    return (top_score, weight_sum, weighted)


def join_parts(first_part, second_part):
    top_score = jnp.maximum(first_part[0], second_part[0])
    left_scale = jnp.exp(first_part[0] - top_score)
    right_scale = jnp.exp(second_part[0] - top_score)
    return (
        top_score,
        first_part[1] * left_scale + second_part[1] * right_scale,
        first_part[2] * left_scale[..., None] + second_part[2] * right_scale[..., None],
    )


def piece_attention(queries, cache_keys, cache_values, lengths, sinks, offset, window):
    req_count, slot_count = (cache_keys.shape[0], cache_keys.shape[1])
    kv_heads, head_dim = (queries.shape[2], queries.shape[4])
    key_rows = cache_keys.reshape(req_count, slot_count, kv_heads, head_dim)
    value_rows = cache_values.reshape(req_count, slot_count, kv_heads, head_dim)
    scores = jnp.einsum(
        "rtkgd,rskd->rkgts", queries, key_rows, preferred_element_type=jnp.float32
    ) * head_dim ** (-0.5)
    cache_pos = offset + jnp.arange(slot_count, dtype=jnp.int32)
    newest_pos = lengths[:, None] + jnp.arange(queries.shape[1], dtype=jnp.int32)[None, :]
    allowed = (cache_pos[None, None, :] < lengths[:, None, None]) & (
        (cache_pos[None, None, :] < sinks[:, None, None])
        | (newest_pos[:, :, None] - cache_pos[None, None, :] < window)
    )
    return softmax_part(scores, allowed[:, None, None, :, :], value_rows, "rkgts,rskd->rkgtd")


def plain_device(
    hidden_in,
    key_cache,
    value_cache,
    cache_len,
    sink_count,
    attn_gain,
    w_query,
    w_key,
    w_value,
    w_headgate,
    q_gain,
    k_gain,
    w_output,
):
    req_count, new_count, model_width = hidden_in.shape
    head_dim = q_gain.shape[0]
    seq_count = lax.axis_size("seq")
    seq_rank = lax.axis_index("seq")
    row_count = req_count * new_count
    window = key_cache.shape[1] * seq_count // 2
    residual = hidden_in.reshape(row_count, model_width).astype(jnp.float32)
    normed = (
        residual
        * lax.rsqrt(jnp.mean(residual * residual, axis=1) + norm_eps)[:, None]
        * attn_gain.astype(jnp.float32)
    ).astype(jnp.bfloat16)
    positions = (cache_len[:, None] + jnp.arange(new_count, dtype=jnp.int32)[None, :]).reshape(
        row_count
    )
    query, new_keys, new_values, head_gate = finish_heads(
        jnp.dot(normed, w_query, preferred_element_type=jnp.float32),
        jnp.dot(normed, w_key, preferred_element_type=jnp.float32),
        jnp.dot(normed, w_value, preferred_element_type=jnp.float32),
        jnp.dot(normed, w_headgate, preferred_element_type=jnp.float32),
        positions,
        q_gain,
        k_gain,
    )
    kv_local = new_keys.shape[1] // head_dim
    q_local = query.shape[1] // head_dim
    per_group = q_local // kv_local
    query_grid = query.reshape(req_count, new_count, kv_local, per_group, head_dim)
    offset = seq_rank * key_cache.shape[1]
    cache_part = piece_attention(
        query_grid, key_cache, value_cache, cache_len, sink_count, offset, window
    )
    top_score = lax.pmax(cache_part[0], "seq")
    rescale = jnp.exp(cache_part[0] - top_score)
    weight_sum, weighted = lax.psum(
        (cache_part[1] * rescale, cache_part[2] * rescale[..., None]), "seq"
    )
    key_grid = new_keys.reshape(req_count, new_count, kv_local, head_dim)
    value_grid = new_values.reshape(req_count, new_count, kv_local, head_dim)
    fresh_scores = jnp.einsum(
        "rtkgd,rjkd->rkgtj", query_grid, key_grid, preferred_element_type=jnp.float32
    ) * head_dim ** (-0.5)
    causal_mask = (
        jnp.arange(new_count, dtype=jnp.int32)[None, :]
        <= jnp.arange(new_count, dtype=jnp.int32)[:, None]
    )
    fresh_part = softmax_part(
        fresh_scores, causal_mask[None, None, None, :, :], value_grid, "rkgtj,rjkd->rkgtd"
    )
    top_score, weight_sum, weighted = join_parts((top_score, weight_sum, weighted), fresh_part)
    attended = weighted / weight_sum[..., None]
    attended = jnp.transpose(attended, (0, 3, 1, 2, 4)).reshape(row_count, q_local, head_dim)
    gated = (
        (attended * head_gate.astype(jnp.float32)[:, :, None])
        .astype(jnp.bfloat16)
        .reshape(row_count, q_local * head_dim)
    )
    column_count = model_width // seq_count
    column_start = seq_rank * column_count
    residual_columns = lax.dynamic_slice_in_dim(residual, column_start, column_count, 1)
    projected = lax.psum(jnp.dot(gated, w_output, preferred_element_type=jnp.float32), "tp")
    projected_columns = lax.dynamic_slice_in_dim(projected, column_start, column_count, 1)
    finished_columns = (residual_columns + projected_columns).astype(jnp.bfloat16)
    return finished_columns.reshape(req_count, new_count, column_count)


def one_hot(flag):
    return jnp.where(flag, 1.0, 0.0).astype(jnp.bfloat16)


def iota(shape, axis):
    return lax.broadcasted_iota(jnp.int32, shape, axis)


def quot(values, size):
    return lax.shift_right_logical(values, size.bit_length() - 1)


def rest(values, size):
    return values & (size - 1)


def head_vectors(sums, gain, cosine, sine):
    scale = lax.rsqrt(jnp.mean(sums * sums, axis=-1, keepdims=True) + norm_eps)
    normed = sums * scale * gain
    turned = normed * cosine + pltpu.roll(normed, sums.shape[1] // 2, 1) * sine
    return turned.astype(jnp.bfloat16)


def attend(scores, allowed):
    top = jnp.max(jnp.where(allowed, scores, masked_fill), axis=-1, keepdims=True)
    weights = jnp.where(allowed, jnp.exp(scores - top), 0.0)
    return top, jnp.sum(weights, axis=-1, keepdims=True), weights.astype(jnp.bfloat16)


def store_part(ref, at, top, total, weighted):
    rows, lanes = weighted.shape
    ref[at, :rows, :] = weighted
    spread = iota((rows, lanes), 1) - iota((rows, lanes), 0)
    stats = jnp.where(spread == 0, top, 0.0) + jnp.where(spread == rows, total, 0.0)
    ref[at, pl.ds(rows, 1), :] = jnp.sum(stats, axis=0, keepdims=True)


query_chunks = 4


def block_kernel(
    new_count, per_group,
    lens_hbm, sinks_hbm, freq_hbm, hidden_hbm, gain_hbm, qg_hbm, kg_hbm, wg_hbm,
    wq_hbm, wk_hbm, wv_hbm, wo_hbm, kc_hbm, vc_hbm,
    out_ref,
    lens_ref, sinks_ref, freq_ref, hidden_ref, gain_ref, qg_ref, kg_ref, wg_ref,
    wq_ref, wk_ref, wv_ref, wo_ref, kc_ref, vc_ref, placed_ref,
    normed_ref, turn_ref, part_ref, got, core_out, core_in, reduced, spread_in, summed, summed_in,
    sems, s_send, s_recv, c_send, c_recv, f_send, f_recv,
):
    rank = lax.axis_index("seq")
    t = lax.axis_index("tp")
    z, y = rank // 2, rank % 2
    x, core = t // 2, t % 2
    crosses = core != y

    order = ((3, 1), (2, 1), (2, 0), (3, 0), (1, 1), (1, 0), (0, 1), (0, 0))
    targets = (0, 1, 3, 2)

    def seq_peer(dz, dy):
        return (z ^ dz) * 2 + (y ^ dy)

    barrier = pltpu.get_barrier_semaphore()

    def greet(seq, tp):
        pl.semaphore_signal(
            barrier, inc=1, device_id={"seq": seq, "tp": tp},
            device_id_type=pl.DeviceIdType.MESH,
        )

    for dz, dy in order[:7]:
        greet(seq_peer(dz, dy), t)
    for i in (2, 3, 1):
        greet(rank, t ^ i)

    loads = {}
    deep = [pl.ds(i * (wq_ref.shape[0] // query_chunks), wq_ref.shape[0] // query_chunks) for i in range(query_chunks)]
    for n, (name, a, b) in enumerate(
        (
            ("lens", lens_hbm, lens_ref), ("freq", freq_hbm, freq_ref),
            ("hidden", hidden_hbm, hidden_ref), ("gain", gain_hbm, gain_ref),
            *(("q%d" % i, wq_hbm.at[at], wq_ref.at[at]) for i, at in enumerate(deep)),
            ("qg", qg_hbm, qg_ref),
            ("sinks", sinks_hbm, sinks_ref), ("kc", kc_hbm, kc_ref), ("vc", vc_hbm, vc_ref),
            ("kg", kg_hbm, kg_ref), ("k", wk_hbm, wk_ref), ("v", wv_hbm, wv_ref),
            ("wg", wg_hbm, wg_ref), ("o", wo_hbm, wo_ref),
        )
    ):
        loads[name] = pltpu.make_async_copy(a, b, sems.at[n])
        loads[name].start()

    def remote(src, dst, send, recv, seq, tp):
        return pltpu.make_async_remote_copy(
            src_ref=src, dst_ref=dst, send_sem=send, recv_sem=recv,
            device_id={"seq": seq, "tp": tp}, device_id_type=pl.DeviceIdType.MESH,
        )

    reqs, slots, width = kc_ref.shape
    rows = reqs * new_count
    hd = freq_ref.shape[1]
    kv_heads = width // hd
    heads = kv_heads * per_group
    each = heads * new_count
    full = reqs * each
    own_reqs = reqs // 8
    own = own_reqs * each
    own_rows = own_reqs * new_count
    window = slots * 8 // 2

    loads["lens"].wait()
    loads["freq"].wait()
    lens = lens_ref[...].astype(jnp.float32)

    def per_row(values, count, size, base):
        chosen = base + quot(iota((count, reqs), 0), size) == iota((count, reqs), 1)
        return jnp.sum(jnp.where(chosen, values, 0.0), axis=1, keepdims=True)

    token = rest(iota((rows, 1), 0), new_count).astype(jnp.float32)
    place = per_row(lens, rows, new_count, 0) + token
    low = iota((rows // 2, hd), 1) < hd // 2
    angle = jnp.where(low, place[: rows // 2], place[rows // 2 :]) * freq_ref[...]

    def unpack(packed, sign):
        turned = pltpu.roll(packed, hd // 2, 1)
        first = jnp.where(low, sign * packed, turned)
        second = jnp.where(low, sign * turned, packed)
        return jnp.concatenate([first, second], axis=0)

    cosine = unpack(jnp.cos(angle), 1.0)
    sine = unpack(jnp.sin(angle), -1.0)

    loads["hidden"].wait()
    loads["gain"].wait()
    hidden = hidden_ref[...].astype(jnp.float32).reshape(rows, hidden_ref.shape[2])
    normed = (
        hidden
        * lax.rsqrt(jnp.mean(hidden * hidden, axis=1, keepdims=True) + norm_eps)
        * gain_ref[...].astype(jnp.float32).reshape(1, -1)
    ).astype(jnp.bfloat16)
    loads["qg"].wait()
    q_gain = qg_ref[...].astype(jnp.float32)
    normed_ref[...] = normed
    turn_ref[0], turn_ref[1] = cosine, sine
    q_sum = jnp.zeros((rows, wq_ref.shape[1]), jnp.float32)
    depth = wq_ref.shape[0] // query_chunks
    for i in range(query_chunks):
        loads["q%d" % i].wait()
        some = slice(i * depth, (i + 1) * depth)
        q_sum = q_sum + jnp.dot(
            normed[:, some], wq_ref[some, :], preferred_element_type=jnp.float32
        )
    query = [
        head_vectors(q_sum[:, h * hd : (h + 1) * hd], q_gain, cosine, sine) for h in range(heads)
    ]
    at = iota((full, rows), 0)
    source = quot(at, each) * new_count + rest(at, new_count)
    hit = source == iota((full, rows), 1)
    head_of = rest(quot(at, new_count), heads)
    for k in range(kv_heads):
        picks = [one_hot(hit & (head_of == k * per_group + g)) for g in range(per_group)]
        moved = jnp.dot(
            jnp.concatenate(picks, axis=1),
            jnp.concatenate(query[k * per_group : (k + 1) * per_group], axis=0),
            preferred_element_type=jnp.float32,
        )
        placed_ref[:, k * hd : (k + 1) * hd] = moved.astype(jnp.bfloat16)

    loads["sinks"].wait()
    sinks = sinks_ref[...].astype(jnp.float32)
    loads["kc"].wait()
    loads["vc"].wait()
    contract = (((1,), (1,)), ((), ()))
    group = each // kv_heads
    pos = rank * slots + iota((own, slots), 1)

    def piece(owner):
        first = owner * own_reqs
        queries = placed_ref[pl.ds(pl.multiple_of(owner * own, own), own), :]
        scores = [
            lax.dot_general(
                queries[r * each : (r + 1) * each],
                kc_ref[first + r],
                contract,
                preferred_element_type=jnp.float32,
            )
            for r in range(own_reqs)
        ]
        scores = jnp.concatenate(scores, axis=0) * hd ** (-0.5)
        length = per_row(lens, own, each, first).astype(jnp.int32)
        sink = per_row(sinks, own, each, first).astype(jnp.int32)
        newest = length + rest(iota((own, 1), 0), new_count)
        allowed = (pos < length) & ((pos < sink) | (newest - pos < window))
        top, total, probs = attend(scores, allowed)
        weighted = []
        for r in range(own_reqs):
            both = jnp.dot(
                probs[r * each : (r + 1) * each],
                vc_ref[first + r],
                preferred_element_type=jnp.float32,
            )
            for k in range(kv_heads):
                weighted.append(both[k * group : (k + 1) * group, k * hd : (k + 1) * hd])
        return top, total, jnp.concatenate(weighted, axis=0)

    passed, joined = order.index((3, 1)), order.index((3, 0))
    swaps = []
    first = 0
    for size in (1, 1, 2, 2, 2):
        chosen = range(first, first + size)
        results = [piece(seq_peer(*order[i])) for i in chosen]
        for i, result in zip(chosen, results):
            store_part(part_ref, i, *result)
        if first == 0:
            pl.semaphore_wait(barrier, 10)
        for i in chosen:
            if i < 7:
                copy = remote(
                    part_ref.at[9 if i == joined else i], got.at[i], s_send.at[i], s_recv.at[i],
                    seq_peer(0, 1) if i == passed else seq_peer(*order[i]), t,
                )
                if i != joined:
                    copy.start()
                swaps.append(copy)
        first += size

    def join(parts):
        stats = [p[own : own + 1, :] for p in parts]
        top = functools.reduce(jnp.maximum, stats)
        scales = [jnp.exp(jnp.minimum(p - top, 0.0)) for p in stats]
        total = functools.reduce(
            jnp.add, [pltpu.roll(p, own, 1) * scale for p, scale in zip(stats, scales)]
        )
        return top, scales, total

    diagonal = iota((own, hd), 1) == iota((own, hd), 0)

    def column(line):
        return jnp.sum(jnp.where(diagonal, line, 0.0), axis=1, keepdims=True)

    def send_joined():
        swaps[passed].wait_recv()
        parts = [part_ref[joined], got[passed]]
        top, scales, total = join(parts)
        part_ref[9, :own, :] = parts[0][:own, :] * column(scales[0]) + parts[1][:own, :] * column(scales[1])
        lanes = iota((1, hd), 1)
        part_ref[9, pl.ds(own, 1), :] = jnp.where(lanes < own, top, pltpu.roll(total, own, 1))
        swaps[joined].start()

    loads["kg"].wait()
    k_gain = kg_ref[...].astype(jnp.float32)
    loads["k"].wait()
    mine_at = pl.ds(pl.multiple_of(rank * own_rows, own_rows), own_rows)
    own_normed = normed_ref[mine_at, :]
    own_cosine, own_sine = turn_ref[0, mine_at, :], turn_ref[1, mine_at, :]
    k_sum = jnp.dot(own_normed, wk_ref[...], preferred_element_type=jnp.float32)
    keys = jnp.concatenate(
        [
            head_vectors(k_sum[:, k * hd : (k + 1) * hd], k_gain, own_cosine, own_sine)
            for k in range(kv_heads)
        ],
        axis=1,
    )
    send_joined()
    loads["v"].wait()
    values = jnp.dot(own_normed, wv_ref[...], preferred_element_type=jnp.float32)
    values = values.astype(jnp.bfloat16)
    mine = placed_ref[pl.ds(pl.multiple_of(rank * own, own), own), :]
    fresh = lax.dot_general(mine, keys, contract, preferred_element_type=jnp.float32)
    fresh = fresh * hd ** (-0.5)
    row = iota((own, own_rows), 0)
    col = iota((own, own_rows), 1)
    own_req = quot(row, each)
    visible = (quot(col, new_count) == own_req) & (rest(col, new_count) <= rest(row, new_count))
    top, total, probs = attend(fresh, visible)
    both = jnp.dot(probs, values, preferred_element_type=jnp.float32)
    row_head = rest(quot(iota((own, hd), 0), new_count), heads)
    picked = jnp.zeros((own, hd), jnp.float32)
    for k in range(kv_heads):
        picked = jnp.where(quot(row_head, per_group) == k, both[:, k * hd : (k + 1) * hd], picked)
    store_part(part_ref, 8, top, total, picked)

    loads["wg"].wait()
    logits = lax.dot_general(own_normed, wg_ref[...], contract, preferred_element_type=jnp.float32)
    gates = jax.nn.sigmoid(logits).astype(jnp.bfloat16)
    pick = one_hot(col == own_req * new_count + rest(row, new_count))
    gates = jnp.dot(pick, gates, preferred_element_type=jnp.float32)
    small = (own, heads)
    gates = jnp.where(rest(quot(iota(small, 0), new_count), heads) == iota(small, 1), gates, 0.0)
    gate = jnp.sum(gates, axis=1, keepdims=True)

    row = iota((own_rows, own), 0)
    col = iota((own_rows, own), 1)
    base = quot(row, new_count) * each + rest(row, new_count)
    back = [one_hot(col == base + h * new_count) for h in range(heads)]
    loads["o"].wait()

    pieces = [part_ref[7], part_ref[8]]
    for i, copy in enumerate(swaps):
        if i != passed:
            copy.wait_recv()
            pieces.append(got[i])
    top, scales, total = join(pieces)
    weighted = jnp.zeros((own, hd), jnp.float32)
    for p, scale in zip(pieces, scales):
        weighted = weighted + p[:own, :] * column(scale / total)
    gated = (weighted * gate).astype(jnp.bfloat16)
    lined = jnp.concatenate(
        [
            jnp.dot(b, gated, preferred_element_type=jnp.float32).astype(jnp.bfloat16)
            for b in back
        ],
        axis=1,
    )
    cols = out_ref.shape[2]

    def project(j, parity):
        start = pl.multiple_of((2 * j + parity) * cols, cols)
        return jnp.dot(lined, wo_ref[:, pl.ds(start, cols)], preferred_element_type=jnp.float32)

    to_core = []
    for half in range(2):
        pair = pl.ds(2 * half, 2)
        for i in (2 * half, 2 * half + 1):
            core_out[i] = project(targets[i], 1 - core)
        copy = remote(
            core_out.at[pair], core_in.at[pair], c_send.at[half], c_recv.at[half], rank, t ^ 1
        )
        copy.start()
        to_core.append(copy)
    for i, target in enumerate(targets):
        reduced[i] = project(target, core)

    spreads = []
    for i, target in enumerate(targets):
        if i in (0, 2):
            to_core[i // 2].wait_recv()
            for j in (i, i + 1):
                reduced[j] = reduced[j] + core_in[j]
        dz = z ^ target
        leaves = crosses | (dz != 0)
        for dx in (1, 0):
            copy = remote(
                reduced.at[i], spread_in.at[dz, dx], f_send.at[2 * i + dx], f_recv.at[2 * dz + dx],
                target * 2 + core, (x ^ dx) * 2 + y,
            )
            spreads.append((copy, None if dx else leaves))
            if dx:
                copy.start()
            else:

                @pl.when(leaves)
                def _():
                    copy.start()

                @pl.when(jnp.logical_not(leaves))
                def _():
                    spread_in[0, 0] = reduced[i]

    column = pl.multiple_of(rank * cols, cols)

    def finish(source_z, parity, block):
        at = pl.ds((source_z * 2 + parity) * own_reqs, own_reqs)
        residual = hidden_ref[at, :, pl.ds(column, cols)].astype(jnp.float32)
        block = block.reshape(own_reqs, new_count, cols)
        out_ref[at] = (residual + block).astype(out_ref.dtype)

    def arrival(dz, dx):
        slot = spread_in.at[dz, dx]
        source = (z ^ dz) * 2 + core, (x ^ dx) * 2 + y
        return remote(slot, slot, f_send.at[0], f_recv.at[2 * dz + dx], *source)

    back_core = []
    for half in range(2):
        pair = pl.ds(2 * half, 2)
        for dz in (2 * half, 2 * half + 1):
            arrival(dz, 1).wait_recv()
            if dz:
                arrival(dz, 0).wait_recv()
            else:

                @pl.when(crosses)
                def _():
                    arrival(0, 0).wait_recv()

            summed[dz] = spread_in[dz, 0] + spread_in[dz, 1]
        copy = remote(
            summed.at[pair], summed_in.at[pair],
            c_send.at[2 + half], c_recv.at[2 + half], rank, t ^ 1,
        )
        copy.start()
        back_core.append(copy)
    for dz in range(4):
        finish(z ^ dz, core, summed[dz])
    for half in range(2):
        back_core[half].wait_recv()
        for dz in (2 * half, 2 * half + 1):
            finish(z ^ dz, 1 - core, summed_in[dz])

    for copy in swaps + to_core + back_core:
        copy.wait_send()
    for copy, leaves in spreads:
        if leaves is None:
            copy.wait_send()
        else:

            @pl.when(leaves)
            def _():
                copy.wait_send()


def fits(seq_count, tp_count, reqs, new_count, heads, slots, hd, model_width):
    own = reqs // seq_count * heads * new_count
    return (
        seq_count == 8
        and tp_count == 4
        and reqs % seq_count == 0
        and model_width % (128 * seq_count) == 0
        and own % 16 == 0
        and 2 * own == hd == slots == 128
        and reqs * new_count == 128
        and heads & (heads - 1) == 0
    )


def per_device(
    hidden_in, key_cache, value_cache, cache_len, sink_count, attn_gain,
    w_query, w_key, w_value, w_headgate, q_gain, k_gain, w_output,
):
    reqs, new_count, model_width = hidden_in.shape
    hd = q_gain.shape[0]
    slots, width = key_cache.shape[1:]
    seq_count = lax.axis_size("seq")
    tp_count = lax.axis_size("tp")
    heads = w_query.shape[1] // hd
    if not fits(seq_count, tp_count, reqs, new_count, heads, slots, hd, model_width):
        return plain_device(
            hidden_in, key_cache, value_cache, cache_len, sink_count, attn_gain,
            w_query, w_key, w_value, w_headgate, q_gain, k_gain, w_output,
        )
    each = heads * new_count
    own = reqs // seq_count * each
    freq = np.tile(rope_theta ** (-np.arange(hd // 2) * 2.0 / hd), 2)[None, :].astype(np.float32)
    f32 = jnp.float32
    own_rows = own // heads
    cols = model_width // seq_count
    sem = pltpu.SemaphoreType.DMA
    operands = (
        cache_len[None, :], sink_count[None, :], freq, hidden_in, attn_gain,
        q_gain[None, :], k_gain[None, :], w_headgate.T,
        w_query, w_key, w_value, w_output, key_cache, value_cache,
    )
    return pl.pallas_call(
        functools.partial(block_kernel, new_count, heads * hd // width),
        out_shape=pltpu.VMEM((reqs, new_count, cols), hidden_in.dtype),
        in_specs=[pl.BlockSpec(memory_space=pl.ANY)] * len(operands),
        out_specs=pl.BlockSpec(memory_space=pltpu.VMEM),
        scratch_shapes=[pltpu.VMEM(a.shape, a.dtype) for a in operands]
        + [
            pltpu.VMEM((reqs * each, width), jnp.bfloat16),
            pltpu.VMEM((reqs * new_count, model_width), jnp.bfloat16),
            pltpu.VMEM((2, reqs * new_count, hd), f32),
            pltpu.VMEM((10, own + 1, hd), f32),
            pltpu.VMEM((7, own + 1, hd), f32),
            pltpu.VMEM((4, own_rows, cols), f32),
            pltpu.VMEM((4, own_rows, cols), f32),
            pltpu.VMEM((4, own_rows, cols), f32),
            pltpu.VMEM((4, 2, own_rows, cols), f32),
            pltpu.VMEM((4, own_rows, cols), f32),
            pltpu.VMEM((4, own_rows, cols), f32),
            sem((len(operands) + query_chunks - 1,)),
            sem((7,)), sem((7,)), sem((4,)), sem((4,)), sem((8,)), sem((8,)),
        ],
        compiler_params=pltpu.CompilerParams(collective_id=0, has_side_effects=True),
        name="attention_block",
    )(*operands)


def solution(mesh):
    placed = (
        P(),
        P(None, "seq", "tp"),
        P(None, "seq", "tp"),
        P(),
        P(),
        P(),
        P(None, "tp"),
        P(None, "tp"),
        P(None, "tp"),
        P(None, "tp"),
        P(),
        P(),
        P("tp", None),
    )
    return jax.shard_map(
        per_device, mesh=mesh, in_specs=placed, out_specs=P(None, None, "seq"), check_vma=False
    )
```

```python
import functools

import jax
import jax.numpy as jnp
import numpy as np
from jax import lax
from jax.experimental import pallas as pl
from jax.experimental.pallas import tpu as pltpu
from jax.sharding import PartitionSpec as P

rope_theta = 1000000.0
norm_eps = 1e-06
masked_fill = -1e30


def rms_scale(values, gain_vec):
    mean_sq = jnp.mean(values * values, axis=-1, keepdims=True)
    return values * lax.rsqrt(mean_sq + norm_eps) * gain_vec.astype(jnp.float32)


def rotate(values, positions):
    half_dim = values.shape[-1] // 2
    inv_freq = rope_theta ** (-jnp.arange(half_dim, dtype=jnp.float32) * 2.0 / values.shape[-1])
    phases = positions.astype(jnp.float32)[:, None] * inv_freq[None, :]
    cosine = jnp.cos(phases)[:, None, :]
    sine_term = jnp.sin(phases)[:, None, :]
    lower_half = values[..., :half_dim]
    upper_half = values[..., half_dim:]
    return jnp.concatenate(
        [
            lower_half * cosine - upper_half * sine_term,
            upper_half * cosine + lower_half * sine_term,
        ],
        axis=-1,
    )


def finish_heads(query, new_keys, new_values, gate_logit, positions, q_gain, k_gain):
    row_count = query.shape[0]
    head_dim = q_gain.shape[0]
    query_heads = rotate(rms_scale(query.reshape(row_count, -1, head_dim), q_gain), positions)
    key_heads = rotate(rms_scale(new_keys.reshape(row_count, -1, head_dim), k_gain), positions)
    return (
        query_heads.reshape(row_count, -1).astype(jnp.bfloat16),
        key_heads.reshape(row_count, -1).astype(jnp.bfloat16),
        new_values.astype(jnp.bfloat16),
        jax.nn.sigmoid(gate_logit).astype(jnp.bfloat16),
    )


def softmax_part(scores, allowed, value_rows, form):
    top_score = jnp.max(jnp.where(allowed, scores, masked_fill), axis=-1)
    weights = jnp.where(allowed, jnp.exp(scores - top_score[..., None]), 0.0)
    weight_sum = jnp.sum(weights, axis=-1)
    weighted = jnp.einsum(
        form, weights.astype(jnp.bfloat16), value_rows, preferred_element_type=jnp.float32
    )
    return (top_score, weight_sum, weighted)


def join_parts(first_part, second_part):
    top_score = jnp.maximum(first_part[0], second_part[0])
    left_scale = jnp.exp(first_part[0] - top_score)
    right_scale = jnp.exp(second_part[0] - top_score)
    return (
        top_score,
        first_part[1] * left_scale + second_part[1] * right_scale,
        first_part[2] * left_scale[..., None] + second_part[2] * right_scale[..., None],
    )


def piece_attention(queries, cache_keys, cache_values, lengths, sinks, offset, window):
    req_count, slot_count = (cache_keys.shape[0], cache_keys.shape[1])
    kv_heads, head_dim = (queries.shape[2], queries.shape[4])
    key_rows = cache_keys.reshape(req_count, slot_count, kv_heads, head_dim)
    value_rows = cache_values.reshape(req_count, slot_count, kv_heads, head_dim)
    scores = jnp.einsum(
        "rtkgd,rskd->rkgts", queries, key_rows, preferred_element_type=jnp.float32
    ) * head_dim ** (-0.5)
    cache_pos = offset + jnp.arange(slot_count, dtype=jnp.int32)
    newest_pos = lengths[:, None] + jnp.arange(queries.shape[1], dtype=jnp.int32)[None, :]
    allowed = (cache_pos[None, None, :] < lengths[:, None, None]) & (
        (cache_pos[None, None, :] < sinks[:, None, None])
        | (newest_pos[:, :, None] - cache_pos[None, None, :] < window)
    )
    return softmax_part(scores, allowed[:, None, None, :, :], value_rows, "rkgts,rskd->rkgtd")


def plain_device(
    hidden_in,
    key_cache,
    value_cache,
    cache_len,
    sink_count,
    attn_gain,
    w_query,
    w_key,
    w_value,
    w_headgate,
    q_gain,
    k_gain,
    w_output,
):
    req_count, new_count, model_width = hidden_in.shape
    head_dim = q_gain.shape[0]
    seq_count = lax.axis_size("seq")
    seq_rank = lax.axis_index("seq")
    row_count = req_count * new_count
    window = key_cache.shape[1] * seq_count // 2
    residual = hidden_in.reshape(row_count, model_width).astype(jnp.float32)
    normed = (
        residual
        * lax.rsqrt(jnp.mean(residual * residual, axis=1) + norm_eps)[:, None]
        * attn_gain.astype(jnp.float32)
    ).astype(jnp.bfloat16)
    positions = (cache_len[:, None] + jnp.arange(new_count, dtype=jnp.int32)[None, :]).reshape(
        row_count
    )
    query, new_keys, new_values, head_gate = finish_heads(
        jnp.dot(normed, w_query, preferred_element_type=jnp.float32),
        jnp.dot(normed, w_key, preferred_element_type=jnp.float32),
        jnp.dot(normed, w_value, preferred_element_type=jnp.float32),
        jnp.dot(normed, w_headgate, preferred_element_type=jnp.float32),
        positions,
        q_gain,
        k_gain,
    )
    kv_local = new_keys.shape[1] // head_dim
    q_local = query.shape[1] // head_dim
    per_group = q_local // kv_local
    query_grid = query.reshape(req_count, new_count, kv_local, per_group, head_dim)
    offset = seq_rank * key_cache.shape[1]
    cache_part = piece_attention(
        query_grid, key_cache, value_cache, cache_len, sink_count, offset, window
    )
    top_score = lax.pmax(cache_part[0], "seq")
    rescale = jnp.exp(cache_part[0] - top_score)
    weight_sum, weighted = lax.psum(
        (cache_part[1] * rescale, cache_part[2] * rescale[..., None]), "seq"
    )
    key_grid = new_keys.reshape(req_count, new_count, kv_local, head_dim)
    value_grid = new_values.reshape(req_count, new_count, kv_local, head_dim)
    fresh_scores = jnp.einsum(
        "rtkgd,rjkd->rkgtj", query_grid, key_grid, preferred_element_type=jnp.float32
    ) * head_dim ** (-0.5)
    causal_mask = (
        jnp.arange(new_count, dtype=jnp.int32)[None, :]
        <= jnp.arange(new_count, dtype=jnp.int32)[:, None]
    )
    fresh_part = softmax_part(
        fresh_scores, causal_mask[None, None, None, :, :], value_grid, "rkgtj,rjkd->rkgtd"
    )
    top_score, weight_sum, weighted = join_parts((top_score, weight_sum, weighted), fresh_part)
    attended = weighted / weight_sum[..., None]
    attended = jnp.transpose(attended, (0, 3, 1, 2, 4)).reshape(row_count, q_local, head_dim)
    gated = (
        (attended * head_gate.astype(jnp.float32)[:, :, None])
        .astype(jnp.bfloat16)
        .reshape(row_count, q_local * head_dim)
    )
    column_count = model_width // seq_count
    column_start = seq_rank * column_count
    residual_columns = lax.dynamic_slice_in_dim(residual, column_start, column_count, 1)
    projected = lax.psum(jnp.dot(gated, w_output, preferred_element_type=jnp.float32), "tp")
    projected_columns = lax.dynamic_slice_in_dim(projected, column_start, column_count, 1)
    finished_columns = (residual_columns + projected_columns).astype(jnp.bfloat16)
    return finished_columns.reshape(req_count, new_count, column_count)


def one_hot(flag):
    return jnp.where(flag, 1.0, 0.0).astype(jnp.bfloat16)


def iota(shape, axis):
    return lax.broadcasted_iota(jnp.int32, shape, axis)


def quot(values, size):
    return lax.shift_right_logical(values, size.bit_length() - 1)


def rest(values, size):
    return values & (size - 1)


def head_vectors(sums, gain, cosine, sine):
    scale = lax.rsqrt(jnp.mean(sums * sums, axis=-1, keepdims=True) + norm_eps)
    normed = sums * scale * gain
    turned = normed * cosine + pltpu.roll(normed, sums.shape[1] // 2, 1) * sine
    return turned.astype(jnp.bfloat16)


def attend(scores, allowed):
    top = jnp.max(jnp.where(allowed, scores, masked_fill), axis=-1, keepdims=True)
    weights = jnp.where(allowed, jnp.exp(scores - top), 0.0)
    return top, jnp.sum(weights, axis=-1, keepdims=True), weights.astype(jnp.bfloat16)


def store_part(ref, at, top, total, weighted):
    rows, lanes = weighted.shape
    ref[at, :rows, :] = weighted
    spread = iota((rows, lanes), 1) - iota((rows, lanes), 0)
    stats = jnp.where(spread == 0, top, 0.0) + jnp.where(spread == rows, total, 0.0)
    ref[at, pl.ds(rows, 1), :] = jnp.sum(stats, axis=0, keepdims=True)


query_chunks = 4


def block_kernel(
    new_count, per_group,
    lens_hbm, sinks_hbm, freq_hbm, hidden_hbm, gain_hbm, qg_hbm, kg_hbm, wg_hbm,
    wq_hbm, wk_hbm, wv_hbm, wo_hbm, kc_hbm, vc_hbm,
    out_ref,
    lens_ref, sinks_ref, freq_ref, hidden_ref, gain_ref, qg_ref, kg_ref, wg_ref,
    wq_ref, wk_ref, wv_ref, wo_ref, kc_ref, vc_ref, placed_ref,
    normed_ref, turn_ref, part_ref, got, core_out, core_in, reduced, spread_in, summed, summed_in,
    sems, s_send, s_recv, c_send, c_recv, f_send, f_recv,
):
    rank = lax.axis_index("seq")
    t = lax.axis_index("tp")
    z, y = rank // 2, rank % 2
    x, core = t // 2, t % 2
    crosses = core != y

    order = ((3, 1), (2, 1), (2, 0), (3, 0), (1, 1), (1, 0), (0, 1), (0, 0))
    targets = (0, 2, 1, 3)
    arrivals = (0, 1, 3, 2)

    def seq_peer(dz, dy):
        return (z ^ dz) * 2 + (y ^ dy)

    barrier = pltpu.get_barrier_semaphore()

    def greet(seq, tp):
        pl.semaphore_signal(
            barrier, inc=1, device_id={"seq": seq, "tp": tp},
            device_id_type=pl.DeviceIdType.MESH,
        )

    loads, late = {}, ("kg", "k", "v", "wg", "o")
    deep = [pl.ds(i * (wq_ref.shape[0] // query_chunks), wq_ref.shape[0] // query_chunks) for i in range(query_chunks)]
    for n, (name, a, b) in enumerate(
        (
            ("hidden", hidden_hbm, hidden_ref), ("lens", lens_hbm, lens_ref),
            ("freq", freq_hbm, freq_ref), ("gain", gain_hbm, gain_ref),
            *(("q%d" % i, wq_hbm.at[at], wq_ref.at[at]) for i, at in enumerate(deep)),
            ("qg", qg_hbm, qg_ref),
            ("sinks", sinks_hbm, sinks_ref), ("kc", kc_hbm, kc_ref), ("vc", vc_hbm, vc_ref),
            ("kg", kg_hbm, kg_ref), ("k", wk_hbm, wk_ref), ("v", wv_hbm, wv_ref),
            ("wg", wg_hbm, wg_ref), ("o", wo_hbm, wo_ref),
        )
    ):
        loads[name] = pltpu.make_async_copy(a, b, sems.at[n])
        if name not in late:
            loads[name].start()

    for dz, dy in order[:7]:
        greet(seq_peer(dz, dy), t)
    for i in (2, 3, 1):
        greet(rank, t ^ i)

    def remote(src, dst, send, recv, seq, tp):
        return pltpu.make_async_remote_copy(
            src_ref=src, dst_ref=dst, send_sem=send, recv_sem=recv,
            device_id={"seq": seq, "tp": tp}, device_id_type=pl.DeviceIdType.MESH,
        )

    reqs, slots, width = kc_ref.shape
    rows = reqs * new_count
    hd = freq_ref.shape[1]
    kv_heads = width // hd
    heads = kv_heads * per_group
    each = heads * new_count
    full = reqs * each
    own_reqs = reqs // 8
    own = own_reqs * each
    own_rows = own_reqs * new_count
    window = slots * 8 // 2

    loads["lens"].wait()
    loads["freq"].wait()
    lens = lens_ref[...].astype(jnp.float32)

    def per_row(values, count, size, base):
        chosen = base + quot(iota((count, reqs), 0), size) == iota((count, reqs), 1)
        return jnp.sum(jnp.where(chosen, values, 0.0), axis=1, keepdims=True)

    token = rest(iota((rows, 1), 0), new_count).astype(jnp.float32)
    place = per_row(lens, rows, new_count, 0) + token
    low = iota((rows // 2, hd), 1) < hd // 2
    angle = jnp.where(low, place[: rows // 2], place[rows // 2 :]) * freq_ref[...]

    def unpack(packed, sign):
        turned = pltpu.roll(packed, hd // 2, 1)
        first = jnp.where(low, sign * packed, turned)
        second = jnp.where(low, sign * turned, packed)
        return jnp.concatenate([first, second], axis=0)

    cosine = unpack(jnp.cos(angle), 1.0)
    sine = unpack(jnp.sin(angle), -1.0)

    loads["hidden"].wait()
    loads["gain"].wait()
    hidden = hidden_ref[...].astype(jnp.float32).reshape(rows, hidden_ref.shape[2])
    normed = (
        hidden
        * lax.rsqrt(jnp.mean(hidden * hidden, axis=1, keepdims=True) + norm_eps)
        * gain_ref[...].astype(jnp.float32).reshape(1, -1)
    ).astype(jnp.bfloat16)
    loads["qg"].wait()
    q_gain = qg_ref[...].astype(jnp.float32)
    normed_ref[...] = normed
    turn_ref[0], turn_ref[1] = cosine, sine
    q_sum = jnp.zeros((rows, wq_ref.shape[1]), jnp.float32)
    depth = wq_ref.shape[0] // query_chunks
    for i in range(query_chunks):
        loads["q%d" % i].wait()
        some = slice(i * depth, (i + 1) * depth)
        q_sum = q_sum + jnp.dot(
            normed[:, some], wq_ref[some, :], preferred_element_type=jnp.float32
        )
    for name in late:
        loads[name].start()
    query = [
        head_vectors(q_sum[:, h * hd : (h + 1) * hd], q_gain, cosine, sine) for h in range(heads)
    ]
    at = iota((full, rows), 0)
    source = quot(at, each) * new_count + rest(at, new_count)
    hit = source == iota((full, rows), 1)
    head_of = rest(quot(at, new_count), heads)
    for k in range(kv_heads):
        picks = [one_hot(hit & (head_of == k * per_group + g)) for g in range(per_group)]
        moved = jnp.dot(
            jnp.concatenate(picks, axis=1),
            jnp.concatenate(query[k * per_group : (k + 1) * per_group], axis=0),
            preferred_element_type=jnp.float32,
        )
        placed_ref[:, k * hd : (k + 1) * hd] = moved.astype(jnp.bfloat16)

    loads["sinks"].wait()
    sinks = sinks_ref[...].astype(jnp.float32)
    loads["kc"].wait()
    loads["vc"].wait()
    contract = (((1,), (1,)), ((), ()))
    group = each // kv_heads
    pos = rank * slots + iota((own, slots), 1)

    def piece(owner):
        first = owner * own_reqs
        queries = placed_ref[pl.ds(pl.multiple_of(owner * own, own), own), :]
        scores = [
            lax.dot_general(
                queries[r * each : (r + 1) * each],
                kc_ref[first + r],
                contract,
                preferred_element_type=jnp.float32,
            )
            for r in range(own_reqs)
        ]
        scores = jnp.concatenate(scores, axis=0) * hd ** (-0.5)
        length = per_row(lens, own, each, first).astype(jnp.int32)
        sink = per_row(sinks, own, each, first).astype(jnp.int32)
        newest = length + rest(iota((own, 1), 0), new_count)
        allowed = (pos < length) & ((pos < sink) | (newest - pos < window))
        top, total, probs = attend(scores, allowed)
        weighted = []
        for r in range(own_reqs):
            both = jnp.dot(
                probs[r * each : (r + 1) * each],
                vc_ref[first + r],
                preferred_element_type=jnp.float32,
            )
            for k in range(kv_heads):
                weighted.append(both[k * group : (k + 1) * group, k * hd : (k + 1) * hd])
        return top, total, jnp.concatenate(weighted, axis=0)

    passed, joined = order.index((3, 1)), order.index((3, 0))
    swaps = []
    first = 0
    for size in (1, 1, 2, 2, 2):
        chosen = range(first, first + size)
        results = [piece(seq_peer(*order[i])) for i in chosen]
        for i, result in zip(chosen, results):
            store_part(part_ref, i, *result)
        if first == 0:
            pl.semaphore_wait(barrier, 10)
        for i in chosen:
            if i < 7:
                copy = remote(
                    part_ref.at[9 if i == joined else i], got.at[i], s_send.at[i], s_recv.at[i],
                    seq_peer(0, 1) if i == passed else seq_peer(*order[i]), t,
                )
                if i != joined:
                    copy.start()
                swaps.append(copy)
        first += size

    def join(parts):
        stats = [p[own : own + 1, :] for p in parts]
        top = functools.reduce(jnp.maximum, stats)
        scales = [jnp.exp(jnp.minimum(p - top, 0.0)) for p in stats]
        total = functools.reduce(
            jnp.add, [pltpu.roll(p, own, 1) * scale for p, scale in zip(stats, scales)]
        )
        return top, scales, total

    diagonal = iota((own, hd), 1) == iota((own, hd), 0)

    def column(line):
        return jnp.sum(jnp.where(diagonal, line, 0.0), axis=1, keepdims=True)

    def send_joined():
        swaps[passed].wait_recv()
        parts = [part_ref[joined], got[passed]]
        top, scales, total = join(parts)
        part_ref[9, :own, :] = functools.reduce(
            jnp.add, [p[:own, :] * column(scale) for p, scale in zip(parts, scales)]
        )
        lanes = iota((1, hd), 1)
        part_ref[9, pl.ds(own, 1), :] = jnp.where(lanes < own, top, pltpu.roll(total, own, 1))
        swaps[joined].start()

    loads["kg"].wait()
    k_gain = kg_ref[...].astype(jnp.float32)
    loads["k"].wait()
    mine_at = pl.ds(pl.multiple_of(rank * own_rows, own_rows), own_rows)
    own_normed = normed_ref[mine_at, :]
    own_cosine, own_sine = turn_ref[0, mine_at, :], turn_ref[1, mine_at, :]
    k_sum = jnp.dot(own_normed, wk_ref[...], preferred_element_type=jnp.float32)
    keys = jnp.concatenate(
        [
            head_vectors(k_sum[:, k * hd : (k + 1) * hd], k_gain, own_cosine, own_sine)
            for k in range(kv_heads)
        ],
        axis=1,
    )
    send_joined()
    loads["v"].wait()
    values = jnp.dot(own_normed, wv_ref[...], preferred_element_type=jnp.float32)
    values = values.astype(jnp.bfloat16)
    mine = placed_ref[pl.ds(pl.multiple_of(rank * own, own), own), :]
    fresh = lax.dot_general(mine, keys, contract, preferred_element_type=jnp.float32)
    fresh = fresh * hd ** (-0.5)
    row = iota((own, own_rows), 0)
    col = iota((own, own_rows), 1)
    own_req = quot(row, each)
    visible = (quot(col, new_count) == own_req) & (rest(col, new_count) <= rest(row, new_count))
    top, total, probs = attend(fresh, visible)
    both = jnp.dot(probs, values, preferred_element_type=jnp.float32)
    row_head = rest(quot(iota((own, hd), 0), new_count), heads)
    picked = jnp.zeros((own, hd), jnp.float32)
    for k in range(kv_heads):
        picked = jnp.where(quot(row_head, per_group) == k, both[:, k * hd : (k + 1) * hd], picked)
    store_part(part_ref, 8, top, total, picked)

    loads["wg"].wait()
    logits = lax.dot_general(own_normed, wg_ref[...], contract, preferred_element_type=jnp.float32)
    gates = jax.nn.sigmoid(logits).astype(jnp.bfloat16)
    pick = one_hot(col == own_req * new_count + rest(row, new_count))
    gates = jnp.dot(pick, gates, preferred_element_type=jnp.float32)
    small = (own, heads)
    gates = jnp.where(rest(quot(iota(small, 0), new_count), heads) == iota(small, 1), gates, 0.0)
    gate = jnp.sum(gates, axis=1, keepdims=True)

    row = iota((own_rows, own), 0)
    col = iota((own_rows, own), 1)
    base = quot(row, new_count) * each + rest(row, new_count)
    back = [one_hot(col == base + h * new_count) for h in range(heads)]
    loads["o"].wait()

    pieces = [part_ref[7], part_ref[8]]
    for i in range(7):
        if i != passed:
            swaps[i].wait_recv()
            pieces.append(got[i])
    top, scales, total = join(pieces)
    weighted = jnp.zeros((own, hd), jnp.float32)
    for p, scale in zip(pieces, scales):
        weighted = weighted + p[:own, :] * column(scale / total)
    gated = (weighted * gate).astype(jnp.bfloat16)
    lined = jnp.concatenate(
        [
            jnp.dot(b, gated, preferred_element_type=jnp.float32).astype(jnp.bfloat16)
            for b in back
        ],
        axis=1,
    )
    cols = out_ref.shape[2]

    def project(j, parity):
        start = pl.multiple_of((2 * j + parity) * cols, cols)
        return jnp.dot(lined, wo_ref[:, pl.ds(start, cols)], preferred_element_type=jnp.float32)

    to_core = []
    for half in range(2):
        pair = pl.ds(2 * half, 2)
        for i in (2 * half, 2 * half + 1):
            core_out[i] = project(targets[i], 1 - core)
        copy = remote(
            core_out.at[pair], core_in.at[pair], c_send.at[half], c_recv.at[half], rank, t ^ 1
        )
        copy.start()
        to_core.append(copy)
    spreads = []
    for i, target in enumerate(targets):
        if i in (0, 2):
            pair = (i, i + 1)
            mine_sums = [project(targets[j], core) for j in pair]
            to_core[i // 2].wait_recv()
            for j, mine_sum in zip(pair, mine_sums):
                reduced[j] = mine_sum + core_in[j]
        dz = z ^ target
        for step in (0, 1):
            dx = x ^ step
            leaves = crosses | (dz != 0) | (dx != 0)
            copy = remote(
                reduced.at[i], spread_in.at[dz, dx], f_send.at[2 * i + step], f_recv.at[2 * dz + dx],
                target * 2 + core, (x ^ dx) * 2 + y,
            )
            spreads.append((copy, leaves))

            @pl.when(leaves)
            def _():
                copy.start()

            @pl.when(jnp.logical_not(leaves))
            def _():
                spread_in[0, 0] = reduced[i]

    column = pl.multiple_of(rank * cols, cols)

    def finish(source_z, parity, block):
        at = pl.ds((source_z * 2 + parity) * own_reqs, own_reqs)
        residual = hidden_ref[at, :, pl.ds(column, cols)].astype(jnp.float32)
        block = block.reshape(own_reqs, new_count, cols)
        out_ref[at] = (residual + block).astype(out_ref.dtype)

    def arrival(dz, dx):
        slot = spread_in.at[dz, dx]
        source = (z ^ dz) * 2 + core, (x ^ dx) * 2 + y
        return remote(slot, slot, f_send.at[0], f_recv.at[2 * dz + dx], *source)

    for copy in swaps + to_core:
        copy.wait_send()

    back_core = []
    size = 2
    for n in range(2):
        for i in range(n * size, (n + 1) * size):
            dz = arrivals[i]
            arrival(dz, 1).wait_recv()
            if dz:
                arrival(dz, 0).wait_recv()
            else:

                @pl.when(crosses)
                def _():
                    arrival(0, 0).wait_recv()

            summed[i] = spread_in[dz, 0] + spread_in[dz, 1]
        at = pl.ds(n * size, size)
        copy = remote(
            summed.at[at], summed_in.at[at], c_send.at[2 + n], c_recv.at[2 + n], rank, t ^ 1
        )
        copy.start()
        back_core.append(copy)
    for i in range(4):
        finish(z ^ arrivals[i], core, summed[i])
    for copy, leaves in spreads:

        @pl.when(leaves)
        def _():
            copy.wait_send()

    for n in range(2):
        back_core[n].wait_recv()
        for i in range(n * size, (n + 1) * size):
            finish(z ^ arrivals[i], 1 - core, summed_in[i])
    for copy in back_core:
        copy.wait_send()


def fits(seq_count, tp_count, reqs, new_count, heads, slots, hd, model_width):
    own = reqs // seq_count * heads * new_count
    return (
        seq_count == 8
        and tp_count == 4
        and reqs % seq_count == 0
        and model_width % (128 * seq_count) == 0
        and own % 16 == 0
        and 2 * own == hd == slots == 128
        and reqs * new_count == 128
        and heads & (heads - 1) == 0
    )


def per_device(
    hidden_in, key_cache, value_cache, cache_len, sink_count, attn_gain,
    w_query, w_key, w_value, w_headgate, q_gain, k_gain, w_output,
):
    reqs, new_count, model_width = hidden_in.shape
    hd = q_gain.shape[0]
    slots, width = key_cache.shape[1:]
    seq_count = lax.axis_size("seq")
    tp_count = lax.axis_size("tp")
    heads = w_query.shape[1] // hd
    if not fits(seq_count, tp_count, reqs, new_count, heads, slots, hd, model_width):
        return plain_device(
            hidden_in, key_cache, value_cache, cache_len, sink_count, attn_gain,
            w_query, w_key, w_value, w_headgate, q_gain, k_gain, w_output,
        )
    each = heads * new_count
    own = reqs // seq_count * each
    freq = np.tile(rope_theta ** (-np.arange(hd // 2) * 2.0 / hd), 2)[None, :].astype(np.float32)
    f32 = jnp.float32
    own_rows = own // heads
    cols = model_width // seq_count
    sem = pltpu.SemaphoreType.DMA
    operands = (
        cache_len[None, :], sink_count[None, :], freq, hidden_in, attn_gain,
        q_gain[None, :], k_gain[None, :], w_headgate.T,
        w_query, w_key, w_value, w_output, key_cache, value_cache,
    )
    return pl.pallas_call(
        functools.partial(block_kernel, new_count, heads * hd // width),
        out_shape=pltpu.VMEM((reqs, new_count, cols), hidden_in.dtype),
        in_specs=[pl.BlockSpec(memory_space=pl.ANY)] * len(operands),
        out_specs=pl.BlockSpec(memory_space=pltpu.VMEM),
        scratch_shapes=[pltpu.VMEM(a.shape, a.dtype) for a in operands]
        + [
            pltpu.VMEM((reqs * each, width), jnp.bfloat16),
            pltpu.VMEM((reqs * new_count, model_width), jnp.bfloat16),
            pltpu.VMEM((2, reqs * new_count, hd), f32),
            pltpu.VMEM((10, own + 1, hd), f32),
            pltpu.VMEM((7, own + 1, hd), f32),
            pltpu.VMEM((4, own_rows, cols), f32),
            pltpu.VMEM((4, own_rows, cols), f32),
            pltpu.VMEM((4, own_rows, cols), f32),
            pltpu.VMEM((4, 2, own_rows, cols), f32),
            pltpu.VMEM((4, own_rows, cols), f32),
            pltpu.VMEM((4, own_rows, cols), f32),
            sem((len(operands) + query_chunks - 1,)),
            sem((7,)), sem((7,)), sem((4,)), sem((4,)), sem((8,)), sem((8,)),
        ],
        compiler_params=pltpu.CompilerParams(collective_id=0, has_side_effects=True),
        name="attention_block",
    )(*operands)


def solution(mesh):
    placed = (
        P(),
        P(None, "seq", "tp"),
        P(None, "seq", "tp"),
        P(),
        P(),
        P(),
        P(None, "tp"),
        P(None, "tp"),
        P(None, "tp"),
        P(None, "tp"),
        P(),
        P(),
        P("tp", None),
    )
    return jax.shard_map(
        per_device, mesh=mesh, in_specs=placed, out_specs=P(None, None, "seq"), check_vma=False
    )
```

```python
import functools

import jax
import jax.numpy as jnp
import numpy as np
from jax import lax
from jax.experimental import pallas as pl
from jax.experimental.pallas import tpu as pltpu
from jax.sharding import PartitionSpec as P

rope_theta = 1000000.0
norm_eps = 1e-06
masked_fill = -1e30


def rms_scale(values, gain_vec):
    mean_sq = jnp.mean(values * values, axis=-1, keepdims=True)
    return values * lax.rsqrt(mean_sq + norm_eps) * gain_vec.astype(jnp.float32)


def rotate(values, positions):
    half_dim = values.shape[-1] // 2
    inv_freq = rope_theta ** (-jnp.arange(half_dim, dtype=jnp.float32) * 2.0 / values.shape[-1])
    phases = positions.astype(jnp.float32)[:, None] * inv_freq[None, :]
    cosine = jnp.cos(phases)[:, None, :]
    sine_term = jnp.sin(phases)[:, None, :]
    lower_half = values[..., :half_dim]
    upper_half = values[..., half_dim:]
    return jnp.concatenate(
        [
            lower_half * cosine - upper_half * sine_term,
            upper_half * cosine + lower_half * sine_term,
        ],
        axis=-1,
    )


def finish_heads(query, new_keys, new_values, gate_logit, positions, q_gain, k_gain):
    row_count = query.shape[0]
    head_dim = q_gain.shape[0]
    query_heads = rotate(rms_scale(query.reshape(row_count, -1, head_dim), q_gain), positions)
    key_heads = rotate(rms_scale(new_keys.reshape(row_count, -1, head_dim), k_gain), positions)
    return (
        query_heads.reshape(row_count, -1).astype(jnp.bfloat16),
        key_heads.reshape(row_count, -1).astype(jnp.bfloat16),
        new_values.astype(jnp.bfloat16),
        jax.nn.sigmoid(gate_logit).astype(jnp.bfloat16),
    )


def softmax_part(scores, allowed, value_rows, form):
    top_score = jnp.max(jnp.where(allowed, scores, masked_fill), axis=-1)
    weights = jnp.where(allowed, jnp.exp(scores - top_score[..., None]), 0.0)
    weight_sum = jnp.sum(weights, axis=-1)
    weighted = jnp.einsum(
        form, weights.astype(jnp.bfloat16), value_rows, preferred_element_type=jnp.float32
    )
    return (top_score, weight_sum, weighted)


def join_parts(first_part, second_part):
    top_score = jnp.maximum(first_part[0], second_part[0])
    left_scale = jnp.exp(first_part[0] - top_score)
    right_scale = jnp.exp(second_part[0] - top_score)
    return (
        top_score,
        first_part[1] * left_scale + second_part[1] * right_scale,
        first_part[2] * left_scale[..., None] + second_part[2] * right_scale[..., None],
    )


def piece_attention(queries, cache_keys, cache_values, lengths, sinks, offset, window):
    req_count, slot_count = (cache_keys.shape[0], cache_keys.shape[1])
    kv_heads, head_dim = (queries.shape[2], queries.shape[4])
    key_rows = cache_keys.reshape(req_count, slot_count, kv_heads, head_dim)
    value_rows = cache_values.reshape(req_count, slot_count, kv_heads, head_dim)
    scores = jnp.einsum(
        "rtkgd,rskd->rkgts", queries, key_rows, preferred_element_type=jnp.float32
    ) * head_dim ** (-0.5)
    cache_pos = offset + jnp.arange(slot_count, dtype=jnp.int32)
    newest_pos = lengths[:, None] + jnp.arange(queries.shape[1], dtype=jnp.int32)[None, :]
    allowed = (cache_pos[None, None, :] < lengths[:, None, None]) & (
        (cache_pos[None, None, :] < sinks[:, None, None])
        | (newest_pos[:, :, None] - cache_pos[None, None, :] < window)
    )
    return softmax_part(scores, allowed[:, None, None, :, :], value_rows, "rkgts,rskd->rkgtd")


def plain_device(
    hidden_in,
    key_cache,
    value_cache,
    cache_len,
    sink_count,
    attn_gain,
    w_query,
    w_key,
    w_value,
    w_headgate,
    q_gain,
    k_gain,
    w_output,
):
    req_count, new_count, model_width = hidden_in.shape
    head_dim = q_gain.shape[0]
    seq_count = lax.axis_size("seq")
    seq_rank = lax.axis_index("seq")
    row_count = req_count * new_count
    window = key_cache.shape[1] * seq_count // 2
    residual = hidden_in.reshape(row_count, model_width).astype(jnp.float32)
    normed = (
        residual
        * lax.rsqrt(jnp.mean(residual * residual, axis=1) + norm_eps)[:, None]
        * attn_gain.astype(jnp.float32)
    ).astype(jnp.bfloat16)
    positions = (cache_len[:, None] + jnp.arange(new_count, dtype=jnp.int32)[None, :]).reshape(
        row_count
    )
    query, new_keys, new_values, head_gate = finish_heads(
        jnp.dot(normed, w_query, preferred_element_type=jnp.float32),
        jnp.dot(normed, w_key, preferred_element_type=jnp.float32),
        jnp.dot(normed, w_value, preferred_element_type=jnp.float32),
        jnp.dot(normed, w_headgate, preferred_element_type=jnp.float32),
        positions,
        q_gain,
        k_gain,
    )
    kv_local = new_keys.shape[1] // head_dim
    q_local = query.shape[1] // head_dim
    per_group = q_local // kv_local
    query_grid = query.reshape(req_count, new_count, kv_local, per_group, head_dim)
    offset = seq_rank * key_cache.shape[1]
    cache_part = piece_attention(
        query_grid, key_cache, value_cache, cache_len, sink_count, offset, window
    )
    top_score = lax.pmax(cache_part[0], "seq")
    rescale = jnp.exp(cache_part[0] - top_score)
    weight_sum, weighted = lax.psum(
        (cache_part[1] * rescale, cache_part[2] * rescale[..., None]), "seq"
    )
    key_grid = new_keys.reshape(req_count, new_count, kv_local, head_dim)
    value_grid = new_values.reshape(req_count, new_count, kv_local, head_dim)
    fresh_scores = jnp.einsum(
        "rtkgd,rjkd->rkgtj", query_grid, key_grid, preferred_element_type=jnp.float32
    ) * head_dim ** (-0.5)
    causal_mask = (
        jnp.arange(new_count, dtype=jnp.int32)[None, :]
        <= jnp.arange(new_count, dtype=jnp.int32)[:, None]
    )
    fresh_part = softmax_part(
        fresh_scores, causal_mask[None, None, None, :, :], value_grid, "rkgtj,rjkd->rkgtd"
    )
    top_score, weight_sum, weighted = join_parts((top_score, weight_sum, weighted), fresh_part)
    attended = weighted / weight_sum[..., None]
    attended = jnp.transpose(attended, (0, 3, 1, 2, 4)).reshape(row_count, q_local, head_dim)
    gated = (
        (attended * head_gate.astype(jnp.float32)[:, :, None])
        .astype(jnp.bfloat16)
        .reshape(row_count, q_local * head_dim)
    )
    column_count = model_width // seq_count
    column_start = seq_rank * column_count
    residual_columns = lax.dynamic_slice_in_dim(residual, column_start, column_count, 1)
    projected = lax.psum(jnp.dot(gated, w_output, preferred_element_type=jnp.float32), "tp")
    projected_columns = lax.dynamic_slice_in_dim(projected, column_start, column_count, 1)
    finished_columns = (residual_columns + projected_columns).astype(jnp.bfloat16)
    return finished_columns.reshape(req_count, new_count, column_count)


def one_hot(flag):
    return jnp.where(flag, 1.0, 0.0).astype(jnp.bfloat16)


def iota(shape, axis):
    return lax.broadcasted_iota(jnp.int32, shape, axis)


def quot(values, size):
    return lax.shift_right_logical(values, size.bit_length() - 1)


def rest(values, size):
    return values & (size - 1)


def head_vectors(sums, gain, cosine, sine):
    scale = lax.rsqrt(jnp.mean(sums * sums, axis=-1, keepdims=True) + norm_eps)
    normed = sums * scale * gain
    turned = normed * cosine + pltpu.roll(normed, sums.shape[1] // 2, 1) * sine
    return turned.astype(jnp.bfloat16)


def attend(scores, allowed):
    top = jnp.max(jnp.where(allowed, scores, masked_fill), axis=-1, keepdims=True)
    weights = jnp.where(allowed, jnp.exp(scores - top), 0.0)
    return top, jnp.sum(weights, axis=-1, keepdims=True), weights.astype(jnp.bfloat16)


def store_part(ref, at, top, total, weighted):
    rows, lanes = weighted.shape
    ref[at, :rows, :] = weighted
    spread = iota((rows, lanes), 1) - iota((rows, lanes), 0)
    stats = jnp.where(spread == 0, top, 0.0) + jnp.where(spread == rows, total, 0.0)
    ref[at, pl.ds(rows, 1), :] = jnp.sum(stats, axis=0, keepdims=True)


query_chunks = 4


def block_kernel(
    new_count, per_group,
    lens_hbm, sinks_hbm, freq_hbm, hidden_hbm, gain_hbm, qg_hbm, kg_hbm, wg_hbm,
    wq_hbm, wk_hbm, wv_hbm, wo_hbm, kc_hbm, vc_hbm,
    out_ref,
    lens_ref, sinks_ref, freq_ref, hidden_ref, gain_ref, qg_ref, kg_ref, wg_ref,
    wq_ref, wk_ref, wv_ref, wo_ref, kc_ref, vc_ref, placed_ref,
    normed_ref, turn_ref, part_ref, got, core_out, core_in, reduced, spread_in, summed, summed_in,
    sems, s_send, s_recv, c_send, c_recv, f_send, f_recv,
):
    rank = lax.axis_index("seq")
    t = lax.axis_index("tp")
    z, y = rank // 2, rank % 2
    x, core = t // 2, t % 2
    crosses = core != y

    order = ((3, 1), (2, 1), (2, 0), (3, 0), (0, 1), (1, 1), (1, 0), (0, 0))
    targets = (0, 2, 1, 3)
    arrivals = (0, 1, 3, 2)

    def seq_peer(dz, dy):
        return (z ^ dz) * 2 + (y ^ dy)

    barrier = pltpu.get_barrier_semaphore()

    def greet(seq, tp):
        pl.semaphore_signal(
            barrier, inc=1, device_id={"seq": seq, "tp": tp},
            device_id_type=pl.DeviceIdType.MESH,
        )

    loads, late = {}, ("kg", "k", "v", "wg", "o")
    deep = [pl.ds(i * (wq_ref.shape[0] // query_chunks), wq_ref.shape[0] // query_chunks) for i in range(query_chunks)]
    for n, (name, a, b) in enumerate(
        (
            ("hidden", hidden_hbm, hidden_ref), ("lens", lens_hbm, lens_ref),
            ("freq", freq_hbm, freq_ref), ("gain", gain_hbm, gain_ref),
            *(("q%d" % i, wq_hbm.at[at], wq_ref.at[at]) for i, at in enumerate(deep)),
            ("qg", qg_hbm, qg_ref),
            ("sinks", sinks_hbm, sinks_ref), ("kc", kc_hbm, kc_ref), ("vc", vc_hbm, vc_ref),
            ("kg", kg_hbm, kg_ref), ("k", wk_hbm, wk_ref), ("v", wv_hbm, wv_ref),
            ("wg", wg_hbm, wg_ref), ("o", wo_hbm, wo_ref),
        )
    ):
        loads[name] = pltpu.make_async_copy(a, b, sems.at[n])
        if name not in late:
            loads[name].start()

    for dz, dy in order[:7]:
        greet(seq_peer(dz, dy), t)
    for i in (2, 3, 1):
        greet(rank, t ^ i)

    def remote(src, dst, send, recv, seq, tp):
        return pltpu.make_async_remote_copy(
            src_ref=src, dst_ref=dst, send_sem=send, recv_sem=recv,
            device_id={"seq": seq, "tp": tp}, device_id_type=pl.DeviceIdType.MESH,
        )

    reqs, slots, width = kc_ref.shape
    rows = reqs * new_count
    hd = freq_ref.shape[1]
    kv_heads = width // hd
    heads = kv_heads * per_group
    each = heads * new_count
    full = reqs * each
    own_reqs = reqs // 8
    own = own_reqs * each
    own_rows = own_reqs * new_count
    window = slots * 8 // 2

    loads["lens"].wait()
    loads["freq"].wait()
    lens = lens_ref[...].astype(jnp.float32)

    def per_row(values, count, size, base):
        chosen = base + quot(iota((count, reqs), 0), size) == iota((count, reqs), 1)
        return jnp.sum(jnp.where(chosen, values, 0.0), axis=1, keepdims=True)

    token = rest(iota((rows, 1), 0), new_count).astype(jnp.float32)
    place = per_row(lens, rows, new_count, 0) + token
    low = iota((rows // 2, hd), 1) < hd // 2
    angle = jnp.where(low, place[: rows // 2], place[rows // 2 :]) * freq_ref[...]

    def unpack(packed, sign):
        turned = pltpu.roll(packed, hd // 2, 1)
        first = jnp.where(low, sign * packed, turned)
        second = jnp.where(low, sign * turned, packed)
        return jnp.concatenate([first, second], axis=0)

    cosine = unpack(jnp.cos(angle), 1.0)
    sine = unpack(jnp.sin(angle), -1.0)

    loads["hidden"].wait()
    loads["gain"].wait()
    hidden = hidden_ref[...].astype(jnp.float32).reshape(rows, hidden_ref.shape[2])
    normed = (
        hidden
        * lax.rsqrt(jnp.mean(hidden * hidden, axis=1, keepdims=True) + norm_eps)
        * gain_ref[...].astype(jnp.float32).reshape(1, -1)
    ).astype(jnp.bfloat16)
    loads["qg"].wait()
    q_gain = qg_ref[...].astype(jnp.float32)
    normed_ref[...] = normed
    turn_ref[0], turn_ref[1] = cosine, sine
    q_sum = jnp.zeros((rows, wq_ref.shape[1]), jnp.float32)
    depth = wq_ref.shape[0] // query_chunks
    for i in range(query_chunks):
        loads["q%d" % i].wait()
        some = slice(i * depth, (i + 1) * depth)
        q_sum = q_sum + jnp.dot(
            normed[:, some], wq_ref[some, :], preferred_element_type=jnp.float32
        )
    for name in late:
        loads[name].start()
    query = [
        head_vectors(q_sum[:, h * hd : (h + 1) * hd], q_gain, cosine, sine) for h in range(heads)
    ]
    at = iota((full, rows), 0)
    source = quot(at, each) * new_count + rest(at, new_count)
    hit = source == iota((full, rows), 1)
    head_of = rest(quot(at, new_count), heads)
    for k in range(kv_heads):
        picks = [one_hot(hit & (head_of == k * per_group + g)) for g in range(per_group)]
        moved = jnp.dot(
            jnp.concatenate(picks, axis=1),
            jnp.concatenate(query[k * per_group : (k + 1) * per_group], axis=0),
            preferred_element_type=jnp.float32,
        )
        placed_ref[:, k * hd : (k + 1) * hd] = moved.astype(jnp.bfloat16)

    loads["sinks"].wait()
    sinks = sinks_ref[...].astype(jnp.float32)
    loads["kc"].wait()
    loads["vc"].wait()
    contract = (((1,), (1,)), ((), ()))
    group = each // kv_heads
    pos = rank * slots + iota((own, slots), 1)

    def piece(owner):
        first = owner * own_reqs
        queries = placed_ref[pl.ds(pl.multiple_of(owner * own, own), own), :]
        scores = [
            lax.dot_general(
                queries[r * each : (r + 1) * each],
                kc_ref[first + r],
                contract,
                preferred_element_type=jnp.float32,
            )
            for r in range(own_reqs)
        ]
        scores = jnp.concatenate(scores, axis=0) * hd ** (-0.5)
        length = per_row(lens, own, each, first).astype(jnp.int32)
        sink = per_row(sinks, own, each, first).astype(jnp.int32)
        newest = length + rest(iota((own, 1), 0), new_count)
        allowed = (pos < length) & ((pos < sink) | (newest - pos < window))
        top, total, probs = attend(scores, allowed)
        weighted = []
        zero = jnp.zeros((each, slots), jnp.bfloat16)
        for r in range(0, own_reqs, 2):
            even, odd = probs[r * each : (r + 1) * each], probs[(r + 1) * each : (r + 2) * each]
            paired = jnp.concatenate(
                [jnp.concatenate([even, zero], axis=1), jnp.concatenate([zero, odd], axis=1)],
                axis=0,
            )
            both = jnp.dot(
                paired,
                vc_ref[pl.ds(first + r, 2)].reshape(2 * slots, width),
                preferred_element_type=jnp.float32,
            )
            for n in range(2 * kv_heads):
                k = n % kv_heads
                weighted.append(both[n * group : (n + 1) * group, k * hd : (k + 1) * hd])
        return top, total, jnp.concatenate(weighted, axis=0)

    passed, joined = order.index((3, 1)), order.index((3, 0))
    swaps = []
    first = 0
    for size in (1, 1, 2, 2, 2):
        chosen = range(first, first + size)
        results = [piece(seq_peer(*order[i])) for i in chosen]
        for i, result in zip(chosen, results):
            store_part(part_ref, i, *result)
        if first == 0:
            pl.semaphore_wait(barrier, 10)
        for i in chosen:
            if i < 7:
                copy = remote(
                    part_ref.at[9 if i == joined else i], got.at[i], s_send.at[i], s_recv.at[i],
                    seq_peer(0, 1) if i == passed else seq_peer(*order[i]), t,
                )
                if i != joined:
                    copy.start()
                swaps.append(copy)
        first += size

    def join(parts):
        stats = [p[own : own + 1, :] for p in parts]
        top = functools.reduce(jnp.maximum, stats)
        scales = [jnp.exp(jnp.minimum(p - top, 0.0)) for p in stats]
        total = functools.reduce(
            jnp.add, [pltpu.roll(p, own, 1) * scale for p, scale in zip(stats, scales)]
        )
        return top, scales, total

    diagonal = iota((own, hd), 1) == iota((own, hd), 0)

    def column(line):
        return jnp.sum(jnp.where(diagonal, line, 0.0), axis=1, keepdims=True)

    def send_joined():
        swaps[passed].wait_recv()
        parts = [part_ref[joined], got[passed]]
        top, scales, total = join(parts)
        part_ref[9, :own, :] = functools.reduce(
            jnp.add, [p[:own, :] * column(scale) for p, scale in zip(parts, scales)]
        )
        lanes = iota((1, hd), 1)
        part_ref[9, pl.ds(own, 1), :] = jnp.where(lanes < own, top, pltpu.roll(total, own, 1))
        swaps[joined].start()

    loads["kg"].wait()
    k_gain = kg_ref[...].astype(jnp.float32)
    loads["k"].wait()
    mine_at = pl.ds(pl.multiple_of(rank * own_rows, own_rows), own_rows)
    own_normed = normed_ref[mine_at, :]
    own_cosine, own_sine = turn_ref[0, mine_at, :], turn_ref[1, mine_at, :]
    k_sum = jnp.dot(own_normed, wk_ref[...], preferred_element_type=jnp.float32)
    keys = jnp.concatenate(
        [
            head_vectors(k_sum[:, k * hd : (k + 1) * hd], k_gain, own_cosine, own_sine)
            for k in range(kv_heads)
        ],
        axis=1,
    )
    send_joined()
    loads["v"].wait()
    values = jnp.dot(own_normed, wv_ref[...], preferred_element_type=jnp.float32)
    values = values.astype(jnp.bfloat16)
    mine = placed_ref[pl.ds(pl.multiple_of(rank * own, own), own), :]
    fresh = lax.dot_general(mine, keys, contract, preferred_element_type=jnp.float32)
    fresh = fresh * hd ** (-0.5)
    row = iota((own, own_rows), 0)
    col = iota((own, own_rows), 1)
    own_req = quot(row, each)
    visible = (quot(col, new_count) == own_req) & (rest(col, new_count) <= rest(row, new_count))
    top, total, probs = attend(fresh, visible)
    both = jnp.dot(probs, values, preferred_element_type=jnp.float32)
    row_head = rest(quot(iota((own, hd), 0), new_count), heads)
    picked = jnp.zeros((own, hd), jnp.float32)
    for k in range(kv_heads):
        picked = jnp.where(quot(row_head, per_group) == k, both[:, k * hd : (k + 1) * hd], picked)
    store_part(part_ref, 8, top, total, picked)

    loads["wg"].wait()
    logits = lax.dot_general(own_normed, wg_ref[...], contract, preferred_element_type=jnp.float32)
    gates = jax.nn.sigmoid(logits).astype(jnp.bfloat16)
    pick = one_hot(col == own_req * new_count + rest(row, new_count))
    gates = jnp.dot(pick, gates, preferred_element_type=jnp.float32)
    small = (own, heads)
    gates = jnp.where(rest(quot(iota(small, 0), new_count), heads) == iota(small, 1), gates, 0.0)
    gate = jnp.sum(gates, axis=1, keepdims=True)

    row = iota((own_rows, own), 0)
    col = iota((own_rows, own), 1)
    base = quot(row, new_count) * each + rest(row, new_count)
    back = [one_hot(col == base + h * new_count) for h in range(heads)]
    loads["o"].wait()

    pieces = [part_ref[7], part_ref[8]]
    for i in range(7):
        if i != passed:
            swaps[i].wait_recv()
            pieces.append(got[i])
    top, scales, total = join(pieces)
    weighted = jnp.zeros((own, hd), jnp.float32)
    for p, scale in zip(pieces, scales):
        weighted = weighted + p[:own, :] * column(scale / total)
    gated = (weighted * gate).astype(jnp.bfloat16)
    lined = jnp.concatenate(
        [
            jnp.dot(b, gated, preferred_element_type=jnp.float32).astype(jnp.bfloat16)
            for b in back
        ],
        axis=1,
    )
    cols = out_ref.shape[2]

    def project(j, parity):
        start = pl.multiple_of((2 * j + parity) * cols, cols)
        return jnp.dot(lined, wo_ref[:, pl.ds(start, cols)], preferred_element_type=jnp.float32)

    to_core = []
    for half in range(2):
        pair = pl.ds(2 * half, 2)
        for i in (2 * half, 2 * half + 1):
            core_out[i] = project(targets[i], 1 - core)
        copy = remote(
            core_out.at[pair], core_in.at[pair], c_send.at[half], c_recv.at[half], rank, t ^ 1
        )
        copy.start()
        to_core.append(copy)
    spreads = []
    for i, target in enumerate(targets):
        if i in (0, 2):
            pair = (i, i + 1)
            mine_sums = [project(targets[j], core) for j in pair]
            to_core[i // 2].wait_recv()
            for j, mine_sum in zip(pair, mine_sums):
                reduced[j] = mine_sum + core_in[j]
        dz = z ^ target
        for step in (0, 1):
            dx = x ^ step
            leaves = crosses | (dz != 0) | (dx != 0)
            copy = remote(
                reduced.at[i], spread_in.at[dz, dx], f_send.at[2 * i + step], f_recv.at[2 * dz + dx],
                target * 2 + core, (x ^ dx) * 2 + y,
            )
            spreads.append((copy, leaves))

            @pl.when(leaves)
            def _():
                copy.start()

            @pl.when(jnp.logical_not(leaves))
            def _():
                spread_in[0, 0] = reduced[i]

    column = pl.multiple_of(rank * cols, cols)

    def finish(source_z, parity, block):
        at = pl.ds((source_z * 2 + parity) * own_reqs, own_reqs)
        residual = hidden_ref[at, :, pl.ds(column, cols)].astype(jnp.float32)
        block = block.reshape(own_reqs, new_count, cols)
        out_ref[at] = (residual + block).astype(out_ref.dtype)

    def arrival(dz, dx):
        slot = spread_in.at[dz, dx]
        source = (z ^ dz) * 2 + core, (x ^ dx) * 2 + y
        return remote(slot, slot, f_send.at[0], f_recv.at[2 * dz + dx], *source)

    for copy in swaps + to_core:
        copy.wait_send()

    back_core = []
    size = 2
    for n in range(2):
        for i in range(n * size, (n + 1) * size):
            dz = arrivals[i]
            arrival(dz, 1).wait_recv()
            if dz:
                arrival(dz, 0).wait_recv()
            else:

                @pl.when(crosses)
                def _():
                    arrival(0, 0).wait_recv()

            summed[i] = spread_in[dz, 0] + spread_in[dz, 1]
        at = pl.ds(n * size, size)
        copy = remote(
            summed.at[at], summed_in.at[at], c_send.at[2 + n], c_recv.at[2 + n], rank, t ^ 1
        )
        copy.start()
        back_core.append(copy)
    for i in range(4):
        finish(z ^ arrivals[i], core, summed[i])
    for copy, leaves in spreads:

        @pl.when(leaves)
        def _():
            copy.wait_send()

    for n in range(2):
        back_core[n].wait_recv()
        for i in range(n * size, (n + 1) * size):
            finish(z ^ arrivals[i], 1 - core, summed_in[i])
    for copy in back_core:
        copy.wait_send()


def fits(seq_count, tp_count, reqs, new_count, heads, slots, hd, model_width):
    own = reqs // seq_count * heads * new_count
    return (
        seq_count == 8
        and tp_count == 4
        and reqs % (2 * seq_count) == 0
        and model_width % (128 * seq_count) == 0
        and own % 16 == 0
        and 2 * own == hd == slots == 128
        and reqs * new_count == 128
        and heads & (heads - 1) == 0
    )


def per_device(
    hidden_in, key_cache, value_cache, cache_len, sink_count, attn_gain,
    w_query, w_key, w_value, w_headgate, q_gain, k_gain, w_output,
):
    reqs, new_count, model_width = hidden_in.shape
    hd = q_gain.shape[0]
    slots, width = key_cache.shape[1:]
    seq_count = lax.axis_size("seq")
    tp_count = lax.axis_size("tp")
    heads = w_query.shape[1] // hd
    if not fits(seq_count, tp_count, reqs, new_count, heads, slots, hd, model_width):
        return plain_device(
            hidden_in, key_cache, value_cache, cache_len, sink_count, attn_gain,
            w_query, w_key, w_value, w_headgate, q_gain, k_gain, w_output,
        )
    each = heads * new_count
    own = reqs // seq_count * each
    freq = np.tile(rope_theta ** (-np.arange(hd // 2) * 2.0 / hd), 2)[None, :].astype(np.float32)
    f32 = jnp.float32
    own_rows = own // heads
    cols = model_width // seq_count
    sem = pltpu.SemaphoreType.DMA
    operands = (
        cache_len[None, :], sink_count[None, :], freq, hidden_in, attn_gain,
        q_gain[None, :], k_gain[None, :], w_headgate.T,
        w_query, w_key, w_value, w_output, key_cache, value_cache,
    )
    return pl.pallas_call(
        functools.partial(block_kernel, new_count, heads * hd // width),
        out_shape=pltpu.VMEM((reqs, new_count, cols), hidden_in.dtype),
        in_specs=[pl.BlockSpec(memory_space=pl.ANY)] * len(operands),
        out_specs=pl.BlockSpec(memory_space=pltpu.VMEM),
        scratch_shapes=[pltpu.VMEM(a.shape, a.dtype) for a in operands]
        + [
            pltpu.VMEM((reqs * each, width), jnp.bfloat16),
            pltpu.VMEM((reqs * new_count, model_width), jnp.bfloat16),
            pltpu.VMEM((2, reqs * new_count, hd), f32),
            pltpu.VMEM((10, own + 1, hd), f32),
            pltpu.VMEM((7, own + 1, hd), f32),
            pltpu.VMEM((4, own_rows, cols), f32),
            pltpu.VMEM((4, own_rows, cols), f32),
            pltpu.VMEM((4, own_rows, cols), f32),
            pltpu.VMEM((4, 2, own_rows, cols), f32),
            pltpu.VMEM((4, own_rows, cols), f32),
            pltpu.VMEM((4, own_rows, cols), f32),
            sem((len(operands) + query_chunks - 1,)),
            sem((7,)), sem((7,)), sem((4,)), sem((4,)), sem((8,)), sem((8,)),
        ],
        compiler_params=pltpu.CompilerParams(collective_id=0, has_side_effects=True),
        name="attention_block",
    )(*operands)


def solution(mesh):
    placed = (
        P(),
        P(None, "seq", "tp"),
        P(None, "seq", "tp"),
        P(),
        P(),
        P(),
        P(None, "tp"),
        P(None, "tp"),
        P(None, "tp"),
        P(None, "tp"),
        P(),
        P(),
        P("tp", None),
    )
    return jax.shard_map(
        per_device, mesh=mesh, in_specs=placed, out_specs=P(None, None, "seq"), check_vma=False
    )
```
